512 devices in a mesh: blk: 512 (over x, z, y, core).
Axes of the slice: x: 4, y: 8, z: 8, core: 2. Of those that a mesh axis runs over, the one named last changes fastest.
Arguments:
- positive_row: float32 [256, 131072], P(None, 'blk'), may hold values from -6 to 160, as said below
- negative_row: float32 [256, 131072], P(None, 'blk'), may hold values from -5 to 5
Outputs:
- positive_out: float32 [256, 131072], P(None, 'blk')
- negative_out: float32 [256, 131072], P(None, 'blk')
The draws below stay inside these ranges and needn't reach their ends.
Inputs may be any that keep to these rules, and one draw needn't show every extreme that they name: `positive_row`: the first 256 columns form an upper triangular block whose diagonal lies between 80 and 160.
All inputs are finite; a program needn't handle non-finite values.
Results may differ from the reference program's by a relative error of at most 0.00017.
Values sent between devices are 32-bit elements; how exact they have to be, the bound alone decides.
No kernel may reach another device: no remote copies, remote signals or barrier semaphores. Data moves between devices by JAX's collectives and lax.ppermute only.
A program may use at most 64 MiB of HBM per device.

```python
import math
import jax
import jax.numpy as jnp
from jax import lax

B = 256
STEPS = 2
NEWTON = 4
ORDER = 131072


def draw_positive_row(key, part):
    key_bulk = jax.random.fold_in(key, 11)
    key_upper = jax.random.fold_in(key, 23)
    key_diag = jax.random.fold_in(key, 37)
    bulk = jnp.clip(0.4 * jax.random.normal(key_bulk, (B, ORDER), jnp.float32), -2.0, 2.0)
    upper = jnp.clip(0.6 * jax.random.normal(key_upper, (B, B), jnp.float32), -2.4, 2.4)
    diagonal = jnp.exp(jax.random.uniform(key_diag, (B,), jnp.float32, math.log(80.0), math.log(160.0)))
    rows_index = jnp.arange(B)[:, None]
    cols_index = jnp.arange(B)[None, :]
    leading = jnp.where(rows_index < cols_index, upper, 0.0) + jnp.where(rows_index == cols_index, diagonal[None, :], 0.0)
    return jnp.concatenate([leading, bulk[:, B:]], axis=1)


def levels(stream_key, extent, pieces, smallest, high):
    def one(axis_at, parts):
        draws = jax.random.uniform(jax.random.fold_in(jax.random.fold_in(stream_key, 6), axis_at), (parts,), jnp.float32, smallest / len(pieces), high / len(pieces))
        return jnp.repeat(jnp.exp(draws), extent[axis_at] // parts).reshape((-1,) + (1,) * (len(extent) - axis_at - 1))

    factor_of = one(*pieces[0])
    for cut in pieces[1:]:
        factor_of = factor_of * one(*cut)
    return factor_of


def normal_values(rng, dims, width, bound, shards=(), kind=jnp.bfloat16):
    entries = jax.random.normal(rng, dims, jnp.float32) * width
    if len(shards) > 0:
        entries = levels(rng, dims, shards, -0.22, 0.18) * entries
    return jnp.clip(entries, min=-bound, max=bound).astype(kind)


def setup_inputs(seed: int = 0) -> dict:
    key_list = jax.random.split(jax.random.key(seed), 3)
    positive_row = draw_positive_row(jax.random.fold_in(key_list[2], 71), 0)
    negative_row = normal_values(key_list[1], (B, ORDER), 0.4, 5.0, ((1, 512),), jnp.float32)
    return dict(positive_row=positive_row, negative_row=negative_row)


HIGHEST = lax.Precision.HIGHEST


def identity_of(size):
    rows_index = lax.broadcasted_iota(jnp.int32, (size, size), 0)
    cols_index = lax.broadcasted_iota(jnp.int32, (size, size), 1)
    return jnp.where(rows_index == cols_index, 1.0, 0.0).astype(jnp.float32)


def root_series(gram_part, identity):
    inner = 0.3125 * identity + 0.2734375 * gram_part
    inner = 0.375 * identity + jnp.dot(gram_part, inner, precision=HIGHEST)
    inner = 0.5 * identity + jnp.dot(gram_part, inner, precision=HIGHEST)
    return identity + jnp.dot(gram_part, inner, precision=HIGHEST)


def build_reflector(lead_p, lead_n):
    identity = identity_of(lead_p.shape[0])
    diag_values = jnp.sum(lead_p * identity, axis=1)
    approx = identity * (1.0 / diag_values)[:, None]
    lead_t = lead_p.T
    for newton_index in range(NEWTON):
        product = jnp.dot(lead_t, approx, precision=HIGHEST)
        approx = jnp.dot(approx, 2.0 * identity - product, precision=HIGHEST)
    coupling_t = jnp.dot(approx, lead_n.T, precision=HIGHEST)
    gram_top = jnp.dot(coupling_t, coupling_t.T, precision=HIGHEST)
    gram_bottom = jnp.dot(coupling_t.T, coupling_t, precision=HIGHEST)
    return coupling_t, root_series(gram_top, identity), root_series(gram_bottom, identity)


def apply_reflector(coupling_t, root_top, root_bottom, positive, negative):
    wide_p = positive - jnp.dot(coupling_t, negative, precision=HIGHEST)
    wide_n = negative - jnp.dot(coupling_t.T, positive, precision=HIGHEST)
    new_p = jnp.dot(root_top, wide_p, precision=HIGHEST)
    new_n = jnp.dot(root_bottom, wide_n, precision=HIGHEST)
    return new_p, new_n


def reference(positive_row, negative_row):
    positive = positive_row
    negative = negative_row
    for step_index in range(STEPS):
        lead_p = positive[:, step_index * B:(step_index + 1) * B]
        lead_n = negative[:, step_index * B:(step_index + 1) * B]
        coupling_t, root_top, root_bottom = build_reflector(lead_p, lead_n)
        new_p, new_n = apply_reflector(coupling_t, root_top, root_bottom, positive, negative)
        positive = jnp.concatenate([jnp.zeros((B, B), jnp.float32), new_p[:, :-B]], axis=1)
        negative = new_n
    return positive, negative
```

```python
import jax
import jax.numpy as jnp
from jax import lax
from jax.experimental import pallas as pl
from jax.experimental.pallas import tpu as pltpu
from jax.sharding import PartitionSpec as P

B = 256
AXIS = "blk"

XS, ZS, YS = 4, 8, 8


def position(x, z, y, core):
    return (((x % XS) * ZS + z % ZS) * YS + y % YS) * 2 + core


TREE = (
    (
        ((2, 0, 0), (-1, 0, 0), (1, 0, 0)),
        ((0, 4, 0), (0, -2, 0), (0, 2, 0)),
        ((0, 0, 4), (0, 0, -2), (0, 0, 2)),
        ((0, 1, 1), (0, 1, 0), (0, 0, 1)),
    ),
    (
        ((0, 4, 0), (0, -2, 0), (0, 2, 0)),
        ((0, 0, 4), (0, 0, -2), (0, 0, 2)),
        ((2, 0, 0), (-1, 0, 0), (1, 0, 0)),
        ((0, -1, -1), (0, -1, 0), (0, 0, -1)),
    ),
)


def tree_rounds():
    holders = [[(0, 0, 0)], [(0, 0, 0)]]
    rounds = []
    for r in range(len(TREE[0])):
        permutes = []
        fresh = [[], []]
        for k in range(len(TREE[0][r])):
            pairs = []
            for core in range(2):
                dx, dz, dy = TREE[core][r][k]
                for x, z, y in holders[core]:
                    to = ((x + dx) % XS, (z + dz) % ZS, (y + dy) % YS)
                    fresh[core].append(to)
                    pairs.append((position(x, z, y, core), position(*to, core)))
            permutes.append(pairs)
        for core in range(2):
            holders[core] += fresh[core]
        rounds.append(permutes)
    return rounds


def halves(a):
    high = a.astype(jnp.bfloat16)
    low = (a - high.astype(jnp.float32)).astype(jnp.bfloat16)
    return high, low


def dot(a, b):
    left = jnp.concatenate([a[0], a[0], a[1]], axis=1)
    right = jnp.concatenate([b[0], b[1], b[0]], axis=0)
    return jnp.dot(left, right, preferred_element_type=jnp.float32)


def eye():
    rows = lax.broadcasted_iota(jnp.int32, (B, B), 0)
    cols = lax.broadcasted_iota(jnp.int32, (B, B), 1)
    return jnp.where(rows == cols, 1.0, 0.0).astype(jnp.float32)


def coupling_of(lead_p, lead_n, identity):
    diag = jnp.sum(lead_p * identity, axis=1, keepdims=True)
    w1 = identity - lead_p * (1.0 / diag)
    h1 = halves(w1)
    w2 = dot(h1, h1)
    m1 = lead_n + dot(halves(lead_n), h1)
    h2 = halves(w2)
    w4 = dot(h2, h2)
    m2 = m1 + dot(halves(m1), h2)
    h4 = halves(w4)
    w8 = dot(h4, h4)
    m3 = m2 + dot(halves(m2), h4)
    m4 = m3 + dot(halves(m3), halves(w8))
    diag_row = jnp.sum(lead_p * identity, axis=0, keepdims=True)
    return m4 * (1.0 / diag_row)


def root_of(gram, identity):
    e = halves(gram)
    square = dot(e, e)
    inner = 0.375 * identity + 0.3125 * gram + 0.2734375 * square
    return identity + 0.5 * gram + dot(halves(square), halves(inner))


def roots_of(k, kt, identity):
    top = root_of(dot(kt, k), identity)
    bottom = root_of(dot(k, kt), identity)
    return halves(top), halves(bottom)


def factor_kernel(me_ref, own_ref, partner_ref, out_ref):
    me = me_ref[0]

    @pl.when(me >= 2)
    def _():
        out_ref[...] = jnp.zeros_like(out_ref)

    @pl.when(me < 2)
    def _():
        identity = eye()
        mine, other = own_ref[...], partner_ref[...]
        first, second = jnp.where(me == 0, mine, other), jnp.where(me == 0, other, mine)
        p0, n0, p1, n1 = first[:B, :], first[B:, :], second[:B, :], second[B:, :]
        k0 = coupling_of(p0, n0, identity)
        k, kt = halves(k0), halves(k0.T)
        top, bottom = roots_of(k, kt, identity)
        lead_p = dot(top, halves(p0 - dot(kt, halves(n0))))
        lead_n = dot(bottom, halves(n1 - dot(k, halves(p1))))
        k1 = coupling_of(lead_p, lead_n, identity)
        out_ref[...] = jnp.where(me == 0, k0, k1)


def apply_kernel(k_ref, back2_ref, back1_ref, own_ref, p_ref, n_ref):
    identity = eye()
    k0, k1 = k_ref[0], k_ref[1]
    h0, t0 = halves(k0), halves(k0.T)
    h1, t1 = halves(k1), halves(k1.T)
    top0, bottom0 = roots_of(h0, t0, identity)
    top1, bottom1 = roots_of(h1, t1, identity)
    p2, n2 = back2_ref[:B, :], back2_ref[B:, :]
    p1, n1 = back1_ref[:B, :], back1_ref[B:, :]
    p0, n0 = own_ref[:B, :], own_ref[B:, :]
    cat = lambda a, b: jnp.concatenate([a, b], axis=1)
    first_p = dot(top0, halves(cat(p2, p1) - dot(t0, halves(cat(n2, n1)))))
    first_n = dot(bottom0, halves(cat(n1, n0) - dot(h0, halves(cat(p1, p0)))))
    p_ref[...] = dot(top1, halves(first_p[:, :B] - dot(t1, halves(first_n[:, :B]))))
    n_ref[...] = dot(bottom1, halves(first_n[:, B:] - dot(h1, halves(first_p[:, B:]))))


VMEM = pl.BlockSpec(memory_space=pltpu.VMEM)
SMEM = pl.BlockSpec(memory_space=pltpu.SMEM)


def on_device(positive_row, negative_row):
    me = lax.axis_index(AXIS)
    devices = lax.axis_size(AXIS)
    cores = [[i, i + 1] for i in range(0, devices, 2)]
    own = jnp.concatenate([positive_row, negative_row], axis=0)
    odd = me % 2 == 1
    swap = [(i, i ^ 1) for i in range(devices)]
    partner = lax.ppermute(own, AXIS, swap)

    route = [(i, i + (1 if i % 2 else 3)) for i in range(devices)]
    crossed = lax.ppermute(own, AXIS, [(i, j) for i, j in route if j < devices])

    factor = pl.pallas_call(
        factor_kernel,
        out_shape=jax.ShapeDtypeStruct((B, B), jnp.float32),
        in_specs=[SMEM, VMEM, VMEM],
        out_specs=VMEM,
    )(jnp.reshape(me, (1,)).astype(jnp.int32), own, partner)

    held = factor
    rounds = tree_rounds()
    for number, permutes in enumerate(rounds):
        if number == len(rounds) - 1:
            held, crossed = lax.optimization_barrier((held, crossed))
            back2 = lax.ppermute(crossed, AXIS, swap)
        arrived = [lax.ppermute(held, AXIS, pairs) for pairs in permutes]
        for block in arrived:
            held = held + block
    back1 = jnp.where(odd, partner, crossed)

    both = lax.all_gather(held, AXIS, axis=0, axis_index_groups=cores)
    return pl.pallas_call(
        apply_kernel,
        out_shape=[jax.ShapeDtypeStruct((B, B), jnp.float32)] * 2,
        in_specs=[VMEM] * 4,
        out_specs=[VMEM] * 2,
    )(both, back2, back1, own)


def solution(mesh):
    spec = P(None, AXIS)
    return jax.shard_map(
        on_device, mesh=mesh, in_specs=(spec, spec), out_specs=(spec, spec), check_vma=False
    )
```

```python
import jax
import jax.numpy as jnp
from jax import lax
from jax.experimental import pallas as pl
from jax.experimental.pallas import tpu as pltpu
from jax.sharding import PartitionSpec as P


B = 256
AXIS = "blk"

XS, ZS, YS = 4, 8, 8


def position(x, z, y, core):
    return (((x % XS) * ZS + z % ZS) * YS + y % YS) * 2 + core


TREE = (
    (
        ((0, -2, 0), (0, -4, 0), (0, 2, 0)),
        ((2, 0, 0), (-1, 0, 0), (1, 0, 0)),
        ((0, 0, 4), (0, 0, -2), (0, 0, 2)),
        ((0, 1, -1), (0, 1, 0), (0, 0, -1)),
    ),
    (
        ((2, 0, 0), (-1, 0, 0), (1, 0, 0)),
        ((0, 0, -4), (0, 0, -2), (0, 0, 2)),
        ((0, 4, 0), (0, -2, 0), (0, 2, 0)),
        ((0, -1, 1), (0, -1, 0), (0, 0, 1)),
    ),
)


def tree_rounds():
    holders = [[(0, 0, 0)], [(0, 0, 0)]]
    rounds = []
    for r in range(len(TREE[0])):
        permutes = []
        fresh = [[], []]
        for k in range(len(TREE[0][r])):
            pairs = []
            for core in range(2):
                dx, dz, dy = TREE[core][r][k]
                for x, z, y in holders[core]:
                    to = ((x + dx) % XS, (z + dz) % ZS, (y + dy) % YS)
                    fresh[core].append(to)
                    pairs.append((position(x, z, y, core), position(*to, core)))
            permutes.append(pairs)
        for core in range(2):
            holders[core] += fresh[core]
        rounds.append(permutes)
    return rounds


def halves(a):
    high = a.astype(jnp.bfloat16)
    low = (a - high.astype(jnp.float32)).astype(jnp.bfloat16)
    return high, low


def dot(a, b):
    left = jnp.concatenate([a[0], a[0], a[1]], axis=1)
    right = jnp.concatenate([b[0], b[1], b[0]], axis=0)
    return jnp.dot(left, right, preferred_element_type=jnp.float32)


def eye():
    rows = lax.broadcasted_iota(jnp.int32, (B, B), 0)
    cols = lax.broadcasted_iota(jnp.int32, (B, B), 1)
    return jnp.where(rows == cols, 1.0, 0.0).astype(jnp.float32)


def coupling_of(lead_p, lead_n, identity):
    diag = jnp.sum(lead_p * identity, axis=1, keepdims=True)
    w1 = identity - lead_p * (1.0 / diag)
    h1 = halves(w1)
    w2 = dot(h1, h1)
    m1 = lead_n + dot(halves(lead_n), h1)
    h2 = halves(w2)
    w4 = dot(h2, h2)
    m2 = m1 + dot(halves(m1), h2)
    h4 = halves(w4)
    w8 = dot(h4, h4)
    m3 = m2 + dot(halves(m2), h4)
    m4 = m3 + dot(halves(m3), halves(w8))
    diag_row = jnp.sum(lead_p * identity, axis=0, keepdims=True)
    return m4 * (1.0 / diag_row)


def root_of(gram, identity):
    e = halves(gram)
    square = dot(e, e)
    inner = 0.375 * identity + 0.3125 * gram + 0.2734375 * square
    return identity + 0.5 * gram + dot(halves(square), halves(inner))


def roots_of(k, kt, identity):
    top = root_of(dot(kt, k), identity)
    bottom = root_of(dot(k, kt), identity)
    return halves(top), halves(bottom)


def stack_kernel(p_ref, n_ref, out_ref, sems):
    copies = [
        pltpu.make_async_copy(p_ref, out_ref.at[:B, :], sems.at[0]),
        pltpu.make_async_copy(n_ref, out_ref.at[B:, :], sems.at[1]),
    ]
    for copy in copies:
        copy.start()
    for copy in copies:
        copy.wait()


def factor_kernel(me_ref, own_ref, next_ref, k0_ref, k1_ref):
    me = me_ref[0]

    @pl.when(me != 0)
    def _():
        k0_ref[...] = jnp.zeros_like(k0_ref)
        k1_ref[...] = jnp.zeros_like(k1_ref)

    @pl.when(me == 0)
    def _():
        identity = eye()
        p0, n0 = own_ref[:B, :], own_ref[B:, :]
        p1, n1 = next_ref[:B, :], next_ref[B:, :]
        k0 = coupling_of(p0, n0, identity)
        k0_ref[...] = k0
        k, kt = halves(k0), halves(k0.T)
        top, bottom = roots_of(k, kt, identity)
        lead_p = dot(top, halves(p0 - dot(kt, halves(n0))))
        lead_n = dot(bottom, halves(n1 - dot(k, halves(p1))))
        k1_ref[...] = coupling_of(lead_p, lead_n, identity)


def apply_kernel(k_ref, back2_ref, back1_ref, own_ref, p_ref, n_ref):
    identity = eye()
    k0, k1 = k_ref[0], k_ref[1]
    h0, t0 = halves(k0), halves(k0.T)
    h1, t1 = halves(k1), halves(k1.T)
    top0, bottom0 = roots_of(h0, t0, identity)
    top1, bottom1 = roots_of(h1, t1, identity)
    p2, n2 = back2_ref[:B, :], back2_ref[B:, :]
    p1, n1 = back1_ref[:B, :], back1_ref[B:, :]
    p0, n0 = own_ref[:B, :], own_ref[B:, :]
    cat = lambda a, b: jnp.concatenate([a, b], axis=1)
    first_p = dot(top0, halves(cat(p2, p1) - dot(t0, halves(cat(n2, n1)))))
    first_n = dot(bottom0, halves(cat(n1, n0) - dot(h0, halves(cat(p1, p0)))))
    p_ref[...] = dot(top1, halves(first_p[:, :B] - dot(t1, halves(first_n[:, :B]))))
    n_ref[...] = dot(bottom1, halves(first_n[:, B:] - dot(h1, halves(first_p[:, B:]))))


VMEM = pl.BlockSpec(memory_space=pltpu.VMEM)
SMEM = pl.BlockSpec(memory_space=pltpu.SMEM)
ANY = pl.BlockSpec(memory_space=pl.ANY)


def resident(*arrays):
    return [pltpu.with_memory_space_constraint(a, pltpu.VMEM) for a in arrays]


def send(array, pairs):
    return lax.ppermute(array, AXIS, pairs)


def steps(positive_row, negative_row):
    me = lax.axis_index(AXIS)
    devices = lax.axis_size(AXIS)
    cores = [[i, i + 1] for i in range(0, devices, 2)]
    onward = [(i, i + 1) for i in range(devices - 1)]
    own = pl.pallas_call(
        stack_kernel,
        out_shape=pltpu.VMEM((2 * B, B), jnp.float32),
        in_specs=[ANY] * 2,
        out_specs=VMEM,
        scratch_shapes=[pltpu.SemaphoreType.DMA((2,))],
    )(positive_row, negative_row)
    second = send(own, [(1, 0)])
    k0, k1 = pl.pallas_call(
        factor_kernel,
        out_shape=[pltpu.VMEM((B, B), jnp.float32)] * 2,
        in_specs=[SMEM, VMEM, VMEM],
        out_specs=[VMEM] * 2,
    )(jnp.reshape(me, (1,)).astype(jnp.int32), *resident(own, second))

    held = k0 + send(k1, [(0, 1)])
    rounds = tree_rounds()
    back1 = send(own, onward)
    back2 = send(back1, onward)
    for permutes in rounds:
        arrived = [send(held, pairs) for pairs in permutes]
        for block in arrived:
            held = held + block

    both = lax.all_gather(held, AXIS, axis=0, axis_index_groups=cores)
    return pl.pallas_call(
        apply_kernel,
        out_shape=[jax.ShapeDtypeStruct((B, B), jnp.float32)] * 2,
        in_specs=[VMEM] * 4,
        out_specs=[VMEM] * 2,
    )(*resident(both, back2, back1, own))


def solution(mesh):
    spec = P(None, AXIS)
    return jax.shard_map(
        steps, mesh=mesh, in_specs=(spec, spec), out_specs=(spec, spec), check_vma=False
    )
```

```python
import jax
import jax.numpy as jnp
from jax import lax
from jax.experimental import pallas as pl
from jax.experimental.pallas import tpu as pltpu
from jax.sharding import PartitionSpec as P


B = 256
AXIS = "blk"

XS, ZS, YS = 4, 8, 8


def position(x, z, y, core):
    return (((x % XS) * ZS + z % ZS) * YS + y % YS) * 2 + core


TREE = (
    (
        ((0, -2, 0), (0, -4, 0), (0, 2, 0)),
        ((2, 0, 0), (-1, 0, 0), (1, 0, 0)),
        ((0, 0, 4), (0, 0, -2), (0, 0, 2)),
        ((0, 1, -1), (0, 1, 0), (0, 0, -1)),
    ),
    (
        ((2, 0, 0), (-1, 0, 0), (1, 0, 0)),
        ((0, 0, -4), (0, 0, -2), (0, 0, 2)),
        ((0, 4, 0), (0, -2, 0), (0, 2, 0)),
        ((0, -1, 1), (0, -1, 0), (0, 0, 1)),
    ),
)


def tree_rounds():
    holders = [[(0, 0, 0)], [(0, 0, 0)]]
    rounds = []
    for r in range(len(TREE[0])):
        permutes = []
        fresh = [[], []]
        for k in range(len(TREE[0][r])):
            pairs = []
            for core in range(2):
                dx, dz, dy = TREE[core][r][k]
                for x, z, y in holders[core]:
                    to = ((x + dx) % XS, (z + dz) % ZS, (y + dy) % YS)
                    fresh[core].append(to)
                    pairs.append((position(x, z, y, core), position(*to, core)))
            permutes.append(pairs)
        for core in range(2):
            holders[core] += fresh[core]
        rounds.append(permutes)
    return rounds


def halves(a):
    high = a.astype(jnp.bfloat16)
    low = (a - high.astype(jnp.float32)).astype(jnp.bfloat16)
    return high, low


def dot(a, b):
    left = jnp.concatenate([a[0], a[0], a[1]], axis=1)
    right = jnp.concatenate([b[0], b[1], b[0]], axis=0)
    return jnp.dot(left, right, preferred_element_type=jnp.float32)


def eye():
    rows = lax.broadcasted_iota(jnp.int32, (B, B), 0)
    cols = lax.broadcasted_iota(jnp.int32, (B, B), 1)
    return jnp.where(rows == cols, 1.0, 0.0).astype(jnp.float32)


def coupling_of(lead_p, lead_n, identity):
    diag = jnp.sum(lead_p * identity, axis=1, keepdims=True)
    w1 = identity - lead_p * (1.0 / diag)
    h1 = halves(w1)
    w2 = dot(h1, h1)
    m1 = lead_n + dot(halves(lead_n), h1)
    h2 = halves(w2)
    w4 = dot(h2, h2)
    m2 = m1 + dot(halves(m1), h2)
    h4 = halves(w4)
    w8 = dot(h4, h4)
    m3 = m2 + dot(halves(m2), h4)
    m4 = m3 + dot(halves(m3), halves(w8))
    diag_row = jnp.sum(lead_p * identity, axis=0, keepdims=True)
    return m4 * (1.0 / diag_row)


def root_of(gram, identity):
    e = halves(gram)
    square = dot(e, e)
    inner = 0.375 * identity + 0.3125 * gram + 0.2734375 * square
    return identity + 0.5 * gram + dot(halves(square), halves(inner))


def roots_of(k, kt, identity):
    top = root_of(dot(kt, k), identity)
    bottom = root_of(dot(k, kt), identity)
    return halves(top), halves(bottom)


def stack_kernel(p_ref, n_ref, out_ref, sems):
    copies = [
        pltpu.make_async_copy(p_ref, out_ref.at[:B, :], sems.at[0]),
        pltpu.make_async_copy(n_ref, out_ref.at[B:, :], sems.at[1]),
    ]
    for copy in copies:
        copy.start()
    for copy in copies:
        copy.wait()


def factor_kernel(me_ref, own_ref, next_ref, k0_ref, k1_ref):
    me = me_ref[0]

    @pl.when(me != 0)
    def _():
        k0_ref[...] = jnp.zeros_like(k0_ref)
        k1_ref[...] = jnp.zeros_like(k1_ref)

    @pl.when(me == 0)
    def _():
        identity = eye()
        p0, n0 = own_ref[:B, :], own_ref[B:, :]
        p1, n1 = next_ref[:B, :], next_ref[B:, :]
        k0 = coupling_of(p0, n0, identity)
        k0_ref[...] = k0
        k, kt = halves(k0), halves(k0.T)
        top, bottom = roots_of(k, kt, identity)
        lead_p = dot(top, halves(p0 - dot(kt, halves(n0))))
        lead_n = dot(bottom, halves(n1 - dot(k, halves(p1))))
        k1_ref[...] = coupling_of(lead_p, lead_n, identity)


def apply_kernel(k_ref, back2_ref, back1_ref, own_ref, p_ref, n_ref):
    identity = eye()
    k0, k1 = k_ref[0], k_ref[1]
    h0, t0 = halves(k0), halves(k0.T)
    h1, t1 = halves(k1), halves(k1.T)
    top0, bottom0 = roots_of(h0, t0, identity)
    top1, bottom1 = roots_of(h1, t1, identity)
    p2, n2 = back2_ref[:B, :], back2_ref[B:, :]
    p1, n1 = back1_ref[:B, :], back1_ref[B:, :]
    p0, n0 = own_ref[:B, :], own_ref[B:, :]
    cat = lambda a, b: jnp.concatenate([a, b], axis=1)
    first_p = dot(top0, halves(cat(p2, p1) - dot(t0, halves(cat(n2, n1)))))
    first_n = dot(bottom0, halves(cat(n1, n0) - dot(h0, halves(cat(p1, p0)))))
    p_ref[...] = dot(top1, halves(first_p[:, :B] - dot(t1, halves(first_n[:, :B]))))
    n_ref[...] = dot(bottom1, halves(first_n[:, B:] - dot(h1, halves(first_p[:, B:]))))


VMEM = pl.BlockSpec(memory_space=pltpu.VMEM)
SMEM = pl.BlockSpec(memory_space=pltpu.SMEM)
ANY = pl.BlockSpec(memory_space=pl.ANY)


def resident(*arrays):
    return [pltpu.with_memory_space_constraint(a, pltpu.VMEM) for a in arrays]


def send(array, pairs):
    return lax.ppermute(array, AXIS, pairs)


def steps(positive_row, negative_row):
    me = lax.axis_index(AXIS)
    devices = lax.axis_size(AXIS)
    cores = [[i, i + 1] for i in range(0, devices, 2)]
    onward = [(i, i + 1) for i in range(1, devices - 1)]
    own = pl.pallas_call(
        stack_kernel,
        out_shape=pltpu.VMEM((2 * B, B), jnp.float32),
        in_specs=[ANY] * 2,
        out_specs=VMEM,
        scratch_shapes=[pltpu.SemaphoreType.DMA((2,))],
    )(positive_row, negative_row)
    second = send(own, [(0, 1), (1, 0)])
    back1 = send(own, onward)
    k0, k1 = pl.pallas_call(
        factor_kernel,
        out_shape=[pltpu.VMEM((B, B), jnp.float32)] * 2,
        in_specs=[SMEM, VMEM, VMEM],
        out_specs=[VMEM] * 2,
    )(jnp.reshape(me, (1,)).astype(jnp.int32), *resident(own, second))

    held = k0 + send(k1, [(0, 1)])
    back1 = jnp.where(me == 1, second, back1)
    back2 = send(back1, onward)
    rounds = tree_rounds()
    for permutes in rounds:
        arrived = [send(held, pairs) for pairs in permutes]
        for block in arrived:
            held = held + block

    both = lax.all_gather(held, AXIS, axis=0, axis_index_groups=cores)
    return pl.pallas_call(
        apply_kernel,
        out_shape=[jax.ShapeDtypeStruct((B, B), jnp.float32)] * 2,
        in_specs=[VMEM] * 4,
        out_specs=[VMEM] * 2,
    )(*resident(both, back2, back1, own))


def solution(mesh):
    spec = P(None, AXIS)
    return jax.shard_map(
        steps, mesh=mesh, in_specs=(spec, spec), out_specs=(spec, spec), check_vma=False
    )
```

```python
import jax
import jax.numpy as jnp
from jax import lax
from jax.experimental import pallas as pl
from jax.experimental.pallas import tpu as pltpu
from jax.sharding import PartitionSpec as P


B = 256
AXIS = "blk"

XS, ZS, YS = 4, 8, 8


def position(x, z, y, core):
    return (((x % XS) * ZS + z % ZS) * YS + y % YS) * 2 + core


TREE = (
    (
        ((0, 0, -4), (0, 0, -2), (0, 0, 2)),
        ((-2, 0, 0), (-1, 0, 0), (1, 0, 0)),
        ((0, 4, 0), (0, -2, 0), (0, 2, 0)),
        ((0, 1, -1), (0, 1, 0), (0, 0, -1)),
    ),
    (
        ((0, -4, 0), (0, -2, 0), (0, 2, 0)),
        ((0, 0, 4), (0, 0, -2), (0, 0, 2)),
        ((-2, 0, 0), (-1, 0, 0), (1, 0, 0)),
        ((0, -1, 1), (0, -1, 0), (0, 0, 1)),
    ),
)


def tree_rounds():
    holders = [[(0, 0, 0)], [(0, 0, 0)]]
    rounds = []
    for r in range(len(TREE[0])):
        permutes = []
        fresh = [[], []]
        for k in range(len(TREE[0][r])):
            pairs = []
            for core in range(2):
                dx, dz, dy = TREE[core][r][k]
                for x, z, y in holders[core]:
                    to = ((x + dx) % XS, (z + dz) % ZS, (y + dy) % YS)
                    fresh[core].append(to)
                    pairs.append((position(x, z, y, core), position(*to, core)))
            permutes.append(pairs)
        for core in range(2):
            holders[core] += fresh[core]
        rounds.append(permutes)
    return rounds


def halves(a):
    high = a.astype(jnp.bfloat16)
    low = (a - high.astype(jnp.float32)).astype(jnp.bfloat16)
    return high, low


def dot(a, b):
    left = jnp.concatenate([a[0], a[0], a[1]], axis=1)
    right = jnp.concatenate([b[0], b[1], b[0]], axis=0)
    return jnp.dot(left, right, preferred_element_type=jnp.float32)


def eye():
    rows = lax.broadcasted_iota(jnp.int32, (B, B), 0)
    cols = lax.broadcasted_iota(jnp.int32, (B, B), 1)
    return jnp.where(rows == cols, 1.0, 0.0).astype(jnp.float32)


def coupling_of(lead_p, lead_n, identity):
    diag = jnp.sum(lead_p * identity, axis=1, keepdims=True)
    w1 = identity - lead_p * (1.0 / diag)
    h1 = halves(w1)
    w2 = dot(h1, h1)
    m1 = lead_n + dot(halves(lead_n), h1)
    h2 = halves(w2)
    w4 = dot(h2, h2)
    m2 = m1 + dot(halves(m1), h2)
    h4 = halves(w4)
    w8 = dot(h4, h4)
    m3 = m2 + dot(halves(m2), h4)
    m4 = m3 + dot(halves(m3), halves(w8))
    diag_row = jnp.sum(lead_p * identity, axis=0, keepdims=True)
    return m4 * (1.0 / diag_row)


def root_of(gram, identity):
    e = halves(gram)
    square = dot(e, e)
    inner = 0.375 * identity + 0.3125 * gram + 0.2734375 * square
    return identity + 0.5 * gram + dot(halves(square), halves(inner))


def roots_of(k, kt, identity):
    top = root_of(dot(kt, k), identity)
    bottom = root_of(dot(k, kt), identity)
    return halves(top), halves(bottom)


def stack_kernel(p_ref, n_ref, out_ref, sems):
    copies = [
        pltpu.make_async_copy(p_ref, out_ref.at[:B, :], sems.at[0]),
        pltpu.make_async_copy(n_ref, out_ref.at[B:, :], sems.at[1]),
    ]
    for copy in copies:
        copy.start()
    for copy in copies:
        copy.wait()


def factor_kernel(me_ref, own_ref, other_ref, out_ref):
    me = me_ref[0]

    @pl.when(me >= 2)
    def _():
        out_ref[...] = jnp.zeros_like(out_ref)

    @pl.when(me < 2)
    def _():
        identity = eye()
        mine, other = own_ref[...], other_ref[...]
        first, second = jnp.where(me == 0, mine, other), jnp.where(me == 0, other, mine)
        p0, n0, p1, n1 = first[:B, :], first[B:, :], second[:B, :], second[B:, :]
        k0 = coupling_of(p0, n0, identity)
        k, kt = halves(k0), halves(k0.T)
        top, bottom = roots_of(k, kt, identity)
        lead_p = dot(top, halves(p0 - dot(kt, halves(n0))))
        lead_n = dot(bottom, halves(n1 - dot(k, halves(p1))))
        k1 = coupling_of(lead_p, lead_n, identity)
        out_ref[...] = jnp.where(me == 0, k0, k1)


def apply_kernel(k_ref, back2_ref, back1_ref, own_ref, p_ref, n_ref):
    identity = eye()
    k0, k1 = k_ref[0], k_ref[1]
    h0, t0 = halves(k0), halves(k0.T)
    h1, t1 = halves(k1), halves(k1.T)
    top0, bottom0 = roots_of(h0, t0, identity)
    top1, bottom1 = roots_of(h1, t1, identity)
    p2, n2 = back2_ref[:B, :], back2_ref[B:, :]
    p1, n1 = back1_ref[:B, :], back1_ref[B:, :]
    p0, n0 = own_ref[:B, :], own_ref[B:, :]
    cat = lambda a, b: jnp.concatenate([a, b], axis=1)
    first_p = dot(top0, halves(cat(p2, p1) - dot(t0, halves(cat(n2, n1)))))
    first_n = dot(bottom0, halves(cat(n1, n0) - dot(h0, halves(cat(p1, p0)))))
    p_ref[...] = dot(top1, halves(first_p[:, :B] - dot(t1, halves(first_n[:, :B]))))
    n_ref[...] = dot(bottom1, halves(first_n[:, B:] - dot(h1, halves(first_p[:, B:]))))


VMEM = pl.BlockSpec(memory_space=pltpu.VMEM)
SMEM = pl.BlockSpec(memory_space=pltpu.SMEM)
ANY = pl.BlockSpec(memory_space=pl.ANY)


def resident(*arrays):
    return [pltpu.with_memory_space_constraint(a, pltpu.VMEM) for a in arrays]


def send(array, pairs):
    return lax.ppermute(array, AXIS, pairs)


def steps(positive_row, negative_row):
    me = lax.axis_index(AXIS)
    devices = lax.axis_size(AXIS)
    cores = [[i, i + 1] for i in range(0, devices, 2)]
    onward = [(i, i + 1) for i in range(1, devices - 1)]
    own = pl.pallas_call(
        stack_kernel,
        out_shape=pltpu.VMEM((2 * B, B), jnp.float32),
        in_specs=[ANY] * 2,
        out_specs=VMEM,
        scratch_shapes=[pltpu.SemaphoreType.DMA((2,))],
    )(positive_row, negative_row)
    second = send(own, [(0, 1), (1, 0)])
    back1 = send(own, onward)
    held = pl.pallas_call(
        factor_kernel,
        out_shape=pltpu.VMEM((B, B), jnp.float32),
        in_specs=[SMEM, VMEM, VMEM],
        out_specs=VMEM,
    )(jnp.reshape(me, (1,)).astype(jnp.int32), *resident(own, second))

    back1 = jnp.where(me == 1, second, back1)
    back2 = send(back1, onward)
    rounds = tree_rounds()
    for permutes in rounds:
        arrived = [send(held, pairs) for pairs in permutes]
        for block in arrived:
            held = held + block

    both = lax.all_gather(held, AXIS, axis=0, axis_index_groups=cores)
    return pl.pallas_call(
        apply_kernel,
        out_shape=[jax.ShapeDtypeStruct((B, B), jnp.float32)] * 2,
        in_specs=[VMEM] * 4,
        out_specs=[VMEM] * 2,
    )(*resident(both, back2, back1, own))


def solution(mesh):
    spec = P(None, AXIS)
    return jax.shard_map(
        steps, mesh=mesh, in_specs=(spec, spec), out_specs=(spec, spec), check_vma=False
    )
```

```python
import jax
import jax.numpy as jnp
from jax import lax
from jax.experimental import pallas as pl
from jax.experimental.pallas import tpu as pltpu
from jax.sharding import PartitionSpec as P


B = 256
AXIS = "blk"

XS, ZS, YS = 4, 8, 8


def position(x, z, y, core):
    return (((x % XS) * ZS + z % ZS) * YS + y % YS) * 2 + core


TREE = (
    (
        ((0, 2, 0), (0, -2, 0), (0, -4, 0)),
        ((0, 0, 4), (0, 0, -2), (0, 0, 2)),
        ((2, 0, 0), (-1, 0, 0), (1, 0, 0)),
        ((0, -1, -1), (0, -1, 0), (0, 0, -1)),
    ),
    (
        ((0, 0, -4), (0, 0, -2), (0, 0, 2)),
        ((0, 2, 0), (0, -2, 0), (0, -4, 0)),
        ((0, -1, -1), (0, -1, 0), (0, 0, -1)),
        ((2, 0, 0), (-1, 0, 0), (1, 0, 0)),
    ),
)


def tree_rounds():
    holders = [[(0, 0, 0)], [(0, 0, 0)]]
    rounds = []
    for r in range(len(TREE[0])):
        permutes = []
        fresh = [[], []]
        for k in range(len(TREE[0][r])):
            pairs = []
            for core in range(2):
                dx, dz, dy = TREE[core][r][k]
                for x, z, y in holders[core]:
                    to = ((x + dx) % XS, (z + dz) % ZS, (y + dy) % YS)
                    fresh[core].append(to)
                    pairs.append((position(x, z, y, core), position(*to, core)))
            permutes.append(pairs)
        for core in range(2):
            holders[core] += fresh[core]
        rounds.append(permutes)
    return rounds


def halves(a):
    high = a.astype(jnp.bfloat16)
    low = (a - high.astype(jnp.float32)).astype(jnp.bfloat16)
    return high, low


def dot(a, b):
    left = jnp.concatenate([a[0], a[0], a[1]], axis=1)
    right = jnp.concatenate([b[0], b[1], b[0]], axis=0)
    return jnp.dot(left, right, preferred_element_type=jnp.float32)


def eye():
    rows = lax.broadcasted_iota(jnp.int32, (B, B), 0)
    cols = lax.broadcasted_iota(jnp.int32, (B, B), 1)
    return jnp.where(rows == cols, 1.0, 0.0).astype(jnp.float32)


def coupling_of(lead_p, lead_n, identity):
    diag = jnp.sum(lead_p * identity, axis=1, keepdims=True)
    w1 = identity - lead_p * (1.0 / diag)
    h1 = halves(w1)
    w2 = dot(h1, h1)
    m1 = lead_n + dot(halves(lead_n), h1)
    h2 = halves(w2)
    w4 = dot(h2, h2)
    m2 = m1 + dot(halves(m1), h2)
    h4 = halves(w4)
    w8 = dot(h4, h4)
    m3 = m2 + dot(halves(m2), h4)
    m4 = m3 + dot(halves(m3), halves(w8))
    diag_row = jnp.sum(lead_p * identity, axis=0, keepdims=True)
    return m4 * (1.0 / diag_row)


def root_of(gram, identity):
    e = halves(gram)
    square = dot(e, e)
    inner = 0.375 * identity + 0.3125 * gram + 0.2734375 * square
    return identity + 0.5 * gram + dot(halves(square), halves(inner))


def roots_of(k, kt, identity):
    top = root_of(dot(kt, k), identity)
    bottom = root_of(dot(k, kt), identity)
    return halves(top), halves(bottom)


def stack_kernel(p_ref, n_ref, out_ref, sems):
    copies = [
        pltpu.make_async_copy(p_ref, out_ref.at[:B, :], sems.at[0]),
        pltpu.make_async_copy(n_ref, out_ref.at[B:, :], sems.at[1]),
    ]
    for copy in copies:
        copy.start()
    for copy in copies:
        copy.wait()


def factor_kernel(me_ref, own_ref, other_ref, out_ref):
    me = me_ref[0]

    @pl.when(me >= 2)
    def _():
        out_ref[...] = jnp.zeros_like(out_ref)

    @pl.when(me < 2)
    def _():
        identity = eye()
        mine, other = own_ref[...], other_ref[...]
        first, second = jnp.where(me == 0, mine, other), jnp.where(me == 0, other, mine)
        p0, n0, p1, n1 = first[:B, :], first[B:, :], second[:B, :], second[B:, :]
        k0 = coupling_of(p0, n0, identity)
        k, kt = halves(k0), halves(k0.T)
        top, bottom = roots_of(k, kt, identity)
        lead_p = dot(top, halves(p0 - dot(kt, halves(n0))))
        lead_n = dot(bottom, halves(n1 - dot(k, halves(p1))))
        k1 = coupling_of(lead_p, lead_n, identity)
        out_ref[...] = jnp.where(me == 0, k0, k1)


def apply_kernel(k_ref, back2_ref, back1_ref, own_ref, p_ref, n_ref):
    identity = eye()
    k0, k1 = k_ref[0], k_ref[1]
    h0, t0 = halves(k0), halves(k0.T)
    h1, t1 = halves(k1), halves(k1.T)
    top0, bottom0 = roots_of(h0, t0, identity)
    top1, bottom1 = roots_of(h1, t1, identity)
    p2, n2 = back2_ref[:B, :], back2_ref[B:, :]
    p1, n1 = back1_ref[:B, :], back1_ref[B:, :]
    p0, n0 = own_ref[:B, :], own_ref[B:, :]
    cat = lambda a, b: jnp.concatenate([a, b], axis=1)
    first_p = dot(top0, halves(cat(p2, p1) - dot(t0, halves(cat(n2, n1)))))
    first_n = dot(bottom0, halves(cat(n1, n0) - dot(h0, halves(cat(p1, p0)))))
    p_ref[...] = dot(top1, halves(first_p[:, :B] - dot(t1, halves(first_n[:, :B]))))
    n_ref[...] = dot(bottom1, halves(first_n[:, B:] - dot(h1, halves(first_p[:, B:]))))


VMEM = pl.BlockSpec(memory_space=pltpu.VMEM)
SMEM = pl.BlockSpec(memory_space=pltpu.SMEM)
ANY = pl.BlockSpec(memory_space=pl.ANY)


def resident(*arrays):
    return [pltpu.with_memory_space_constraint(a, pltpu.VMEM) for a in arrays]


def send(array, pairs):
    return lax.ppermute(array, AXIS, pairs)


def steps(positive_row, negative_row):
    me = lax.axis_index(AXIS)
    devices = lax.axis_size(AXIS)
    cores = [[i, i + 1] for i in range(0, devices, 2)]
    onward = [(i, i + 1) for i in range(1, devices - 1)]
    own = pl.pallas_call(
        stack_kernel,
        out_shape=pltpu.VMEM((2 * B, B), jnp.float32),
        in_specs=[ANY] * 2,
        out_specs=VMEM,
        scratch_shapes=[pltpu.SemaphoreType.DMA((2,))],
    )(positive_row, negative_row)
    second = send(own, [(0, 1), (1, 0)])
    back1 = send(own, onward)
    held = pl.pallas_call(
        factor_kernel,
        out_shape=pltpu.VMEM((B, B), jnp.float32),
        in_specs=[SMEM, VMEM, VMEM],
        out_specs=VMEM,
    )(jnp.reshape(me, (1,)).astype(jnp.int32), *resident(own, second))

    back1 = jnp.where(me == 1, second, back1)
    back2 = send(back1, onward)
    rounds = tree_rounds()
    for permutes in rounds:
        arrived = [send(held, pairs) for pairs in permutes]
        for block in arrived:
            held = held + block

    both = lax.all_gather(held, AXIS, axis=0, axis_index_groups=cores)
    return pl.pallas_call(
        apply_kernel,
        out_shape=[jax.ShapeDtypeStruct((B, B), jnp.float32)] * 2,
        in_specs=[VMEM] * 4,
        out_specs=[VMEM] * 2,
    )(*resident(both, back2, back1, own))


def solution(mesh):
    spec = P(None, AXIS)
    return jax.shard_map(
        steps, mesh=mesh, in_specs=(spec, spec), out_specs=(spec, spec), check_vma=False
    )
```

```python
import jax
import jax.numpy as jnp
from jax import lax
from jax.experimental import pallas as pl
from jax.experimental.pallas import tpu as pltpu
from jax.sharding import PartitionSpec as P


B = 256
AXIS = "blk"

XS, ZS, YS = 4, 8, 8


def position(x, z, y, core):
    return (((x % XS) * ZS + z % ZS) * YS + y % YS) * 2 + core


TREE = (
    (
        ((0, 0, 2), (0, 0, -2), (0, 0, 4)),
        ((0, 2, 0), (0, -2, 0), (0, 4, 0)),
        ((1, 0, 0), (-1, 0, 0), (2, 0, 0)),
        ((0, 1, -1), (0, 1, 0), (0, 0, -1)),
    ),
    (
        ((1, 0, 0), (-1, 0, 0), (2, 0, 0)),
        ((0, 0, 2), (0, 0, -2), (0, 0, 4)),
        ((0, 2, 0), (0, -2, 0), (0, 4, 0)),
        ((0, -1, 1), (0, -1, 0), (0, 0, 1)),
    ),
)


def tree_rounds():
    holders = [[(0, 0, 0)], [(0, 0, 0)]]
    rounds = []
    for r in range(len(TREE[0])):
        permutes = []
        fresh = [[], []]
        for k in range(len(TREE[0][r])):
            pairs = []
            for core in range(2):
                dx, dz, dy = TREE[core][r][k]
                for x, z, y in holders[core]:
                    to = ((x + dx) % XS, (z + dz) % ZS, (y + dy) % YS)
                    fresh[core].append(to)
                    pairs.append((position(x, z, y, core), position(*to, core)))
            permutes.append(pairs)
        for core in range(2):
            holders[core] += fresh[core]
        rounds.append(permutes)
    return rounds


def halves(a):
    high = a.astype(jnp.bfloat16)
    low = (a - high.astype(jnp.float32)).astype(jnp.bfloat16)
    return high, low


def dot(a, b):
    left = jnp.concatenate([a[0], a[0], a[1]], axis=1)
    right = jnp.concatenate([b[0], b[1], b[0]], axis=0)
    return jnp.dot(left, right, preferred_element_type=jnp.float32)


def eye():
    rows = lax.broadcasted_iota(jnp.int32, (B, B), 0)
    cols = lax.broadcasted_iota(jnp.int32, (B, B), 1)
    return jnp.where(rows == cols, 1.0, 0.0).astype(jnp.float32)


def coupling_of(lead_p, lead_n, identity):
    diag = jnp.sum(lead_p * identity, axis=1, keepdims=True)
    w1 = identity - lead_p * (1.0 / diag)
    h1 = halves(w1)
    w2 = dot(h1, h1)
    m1 = lead_n + dot(halves(lead_n), h1)
    h2 = halves(w2)
    w4 = dot(h2, h2)
    m2 = m1 + dot(halves(m1), h2)
    h4 = halves(w4)
    w8 = dot(h4, h4)
    m3 = m2 + dot(halves(m2), h4)
    m4 = m3 + dot(halves(m3), halves(w8))
    diag_row = jnp.sum(lead_p * identity, axis=0, keepdims=True)
    return m4 * (1.0 / diag_row)


def root_of(gram, identity):
    e = halves(gram)
    square = dot(e, e)
    inner = 0.375 * identity + 0.3125 * gram + 0.2734375 * square
    return identity + 0.5 * gram + dot(halves(square), halves(inner))


def roots_of(k, kt, identity):
    top = root_of(dot(kt, k), identity)
    bottom = root_of(dot(k, kt), identity)
    return halves(top), halves(bottom)


def stack_kernel(p_ref, n_ref, out_ref, sems):
    copies = [
        pltpu.make_async_copy(p_ref, out_ref.at[:B, :], sems.at[0]),
        pltpu.make_async_copy(n_ref, out_ref.at[B:, :], sems.at[1]),
    ]
    for copy in copies:
        copy.start()
    for copy in copies:
        copy.wait()


def factor_kernel(me_ref, own_ref, other_ref, out_ref):
    me = me_ref[0]

    @pl.when(me >= 2)
    def _():
        out_ref[...] = jnp.zeros_like(out_ref)

    @pl.when(me < 2)
    def _():
        identity = eye()
        mine, other = own_ref[...], other_ref[...]
        first, second = jnp.where(me == 0, mine, other), jnp.where(me == 0, other, mine)
        p0, n0, p1, n1 = first[:B, :], first[B:, :], second[:B, :], second[B:, :]
        k0 = coupling_of(p0, n0, identity)
        k, kt = halves(k0), halves(k0.T)
        top, bottom = roots_of(k, kt, identity)
        lead_p = dot(top, halves(p0 - dot(kt, halves(n0))))
        lead_n = dot(bottom, halves(n1 - dot(k, halves(p1))))
        k1 = coupling_of(lead_p, lead_n, identity)
        out_ref[...] = jnp.where(me == 0, k0, k1)


def apply_kernel(k_ref, back2_ref, back1_ref, own_ref, p_ref, n_ref):
    identity = eye()
    k0, k1 = k_ref[0], k_ref[1]
    h0, t0 = halves(k0), halves(k0.T)
    h1, t1 = halves(k1), halves(k1.T)
    top0, bottom0 = roots_of(h0, t0, identity)
    top1, bottom1 = roots_of(h1, t1, identity)
    p2, n2 = back2_ref[:B, :], back2_ref[B:, :]
    p1, n1 = back1_ref[:B, :], back1_ref[B:, :]
    p0, n0 = own_ref[:B, :], own_ref[B:, :]
    cat = lambda a, b: jnp.concatenate([a, b], axis=1)
    first_p = dot(top0, halves(cat(p2, p1) - dot(t0, halves(cat(n2, n1)))))
    first_n = dot(bottom0, halves(cat(n1, n0) - dot(h0, halves(cat(p1, p0)))))
    p_ref[...] = dot(top1, halves(first_p[:, :B] - dot(t1, halves(first_n[:, :B]))))
    n_ref[...] = dot(bottom1, halves(first_n[:, B:] - dot(h1, halves(first_p[:, B:]))))


VMEM = pl.BlockSpec(memory_space=pltpu.VMEM)
SMEM = pl.BlockSpec(memory_space=pltpu.SMEM)
ANY = pl.BlockSpec(memory_space=pl.ANY)


def resident(*arrays):
    return [pltpu.with_memory_space_constraint(a, pltpu.VMEM) for a in arrays]


def send(array, pairs):
    return lax.ppermute(array, AXIS, pairs)


def steps(positive_row, negative_row):
    me = lax.axis_index(AXIS)
    devices = lax.axis_size(AXIS)
    cores = [[i, i + 1] for i in range(0, devices, 2)]
    onward = [(i, i + 1) for i in range(1, devices - 1)]
    own = pl.pallas_call(
        stack_kernel,
        out_shape=pltpu.VMEM((2 * B, B), jnp.float32),
        in_specs=[ANY] * 2,
        out_specs=VMEM,
        scratch_shapes=[pltpu.SemaphoreType.DMA((2,))],
    )(positive_row, negative_row)
    second = send(own, [(0, 1), (1, 0)])
    back1 = send(own, onward)
    held = pl.pallas_call(
        factor_kernel,
        out_shape=pltpu.VMEM((B, B), jnp.float32),
        in_specs=[SMEM, VMEM, VMEM],
        out_specs=VMEM,
    )(jnp.reshape(me, (1,)).astype(jnp.int32), *resident(own, second))

    back2 = send(jnp.where(me == 0, own, back1), [(0, 2)] + onward[1:])
    back1 = jnp.where(me == 1, second, back1)
    rounds = tree_rounds()
    for permutes in rounds:
        arrived = [send(held, pairs) for pairs in permutes]
        for block in arrived:
            held = held + block

    both = lax.all_gather(held, AXIS, axis=0, axis_index_groups=cores)
    return pl.pallas_call(
        apply_kernel,
        out_shape=[jax.ShapeDtypeStruct((B, B), jnp.float32)] * 2,
        in_specs=[VMEM] * 4,
        out_specs=[VMEM] * 2,
    )(*resident(both, back2, back1, own))


def solution(mesh):
    spec = P(None, AXIS)
    return jax.shard_map(
        steps, mesh=mesh, in_specs=(spec, spec), out_specs=(spec, spec), check_vma=False
    )
```

```python
import jax
import jax.numpy as jnp
from jax import lax
from jax.experimental import pallas as pl
from jax.experimental.pallas import tpu as pltpu
from jax.sharding import PartitionSpec as P


B = 256
AXIS = "blk"

XS, ZS, YS = 4, 8, 8


def position(x, z, y, core):
    return (((x % XS) * ZS + z % ZS) * YS + y % YS) * 2 + core


TREE = (
    (
        ((2, 0, 0), (-1, 0, 0), (1, 0, 0)),
        ((0, 0, 2), (0, 0, -2), (0, 0, 4)),
        ((0, 2, 0), (0, -2, 0), (0, 4, 0)),
        ((0, 0, 1), (0, -1, 0), (0, -1, 1)),
    ),
    (
        ((0, 0, 2), (0, 0, -2), (0, 0, 4)),
        ((0, 2, 0), (0, -2, 0), (0, 4, 0)),
        ((1, 0, 0), (-1, 0, 0), (2, 0, 0)),
        ((0, 0, -1), (0, 1, 0), (0, 1, -1)),
    ),
)


def tree_rounds():
    holders = [[(0, 0, 0)], [(0, 0, 0)]]
    rounds = []
    for r in range(len(TREE[0])):
        permutes = []
        fresh = [[], []]
        for k in range(len(TREE[0][r])):
            pairs = []
            for core in range(2):
                dx, dz, dy = TREE[core][r][k]
                for x, z, y in holders[core]:
                    to = ((x + dx) % XS, (z + dz) % ZS, (y + dy) % YS)
                    fresh[core].append(to)
                    pairs.append((position(x, z, y, core), position(*to, core)))
            permutes.append(pairs)
        for core in range(2):
            holders[core] += fresh[core]
        rounds.append(permutes)
    return rounds


def halves(a):
    high = a.astype(jnp.bfloat16)
    low = (a - high.astype(jnp.float32)).astype(jnp.bfloat16)
    return high, low


def dot(a, b):
    rows = a[0].shape[0]
    both = jnp.dot(jnp.concatenate([a[0], a[1]], axis=0), b[0], preferred_element_type=jnp.float32)
    cross = jnp.dot(a[0], b[1], preferred_element_type=jnp.float32)
    return both[:rows] + (both[rows:] + cross)


def eye():
    rows = lax.broadcasted_iota(jnp.int32, (B, B), 0)
    cols = lax.broadcasted_iota(jnp.int32, (B, B), 1)
    return jnp.where(rows == cols, 1.0, 0.0).astype(jnp.float32)


def coupling_of(lead_p, lead_n, identity):
    diag = jnp.sum(lead_p * identity, axis=1, keepdims=True)
    w1 = identity - lead_p * (1.0 / diag)
    h1 = halves(w1)
    w2 = dot(h1, h1)
    m1 = lead_n + dot(halves(lead_n), h1)
    h2 = halves(w2)
    w4 = dot(h2, h2)
    m2 = m1 + dot(halves(m1), h2)
    h4 = halves(w4)
    w8 = dot(h4, h4)
    m3 = m2 + dot(halves(m2), h4)
    m4 = m3 + dot(halves(m3), halves(w8))
    diag_row = jnp.sum(lead_p * identity, axis=0, keepdims=True)
    return m4 * (1.0 / diag_row)


def root_of(gram, identity):
    e = halves(gram)
    square = dot(e, e)
    inner = 0.375 * identity + 0.3125 * gram + 0.2734375 * square
    return identity + 0.5 * gram + dot(halves(square), halves(inner))


def roots_of(k, kt, identity):
    top = root_of(dot(kt, k), identity)
    bottom = root_of(dot(k, kt), identity)
    return halves(top), halves(bottom)


def stack_kernel(p_ref, n_ref, out_ref, sems):
    copies = [
        pltpu.make_async_copy(p_ref, out_ref.at[:B, :], sems.at[0]),
        pltpu.make_async_copy(n_ref, out_ref.at[B:, :], sems.at[1]),
    ]
    for copy in copies:
        copy.start()
    for copy in copies:
        copy.wait()


def factor_kernel(me_ref, own_ref, other_ref, out_ref):
    me = me_ref[0]

    @pl.when(me >= 2)
    def _():
        out_ref[...] = jnp.zeros_like(out_ref)

    @pl.when(me < 2)
    def _():
        identity = eye()
        mine, other = own_ref[...], other_ref[...]
        first, second = jnp.where(me == 0, mine, other), jnp.where(me == 0, other, mine)
        p0, n0, p1, n1 = first[:B, :], first[B:, :], second[:B, :], second[B:, :]
        k0 = coupling_of(p0, n0, identity)
        k, kt = halves(k0), halves(k0.T)
        top, bottom = roots_of(k, kt, identity)
        lead_p = dot(top, halves(p0 - dot(kt, halves(n0))))
        lead_n = dot(bottom, halves(n1 - dot(k, halves(p1))))
        k1 = coupling_of(lead_p, lead_n, identity)
        out_ref[...] = jnp.where(me == 0, k0, k1)


def apply_kernel(k_ref, back2_ref, back1_ref, own_ref, p_ref, n_ref):
    identity = eye()
    k0, k1 = k_ref[0], k_ref[1]
    h0, t0 = halves(k0), halves(k0.T)
    h1, t1 = halves(k1), halves(k1.T)
    top0, bottom0 = roots_of(h0, t0, identity)
    top1, bottom1 = roots_of(h1, t1, identity)
    p2, n2 = back2_ref[:B, :], back2_ref[B:, :]
    p1, n1 = back1_ref[:B, :], back1_ref[B:, :]
    p0, n0 = own_ref[:B, :], own_ref[B:, :]
    cat = lambda a, b: jnp.concatenate([a, b], axis=1)
    first_p = dot(top0, halves(cat(p2, p1) - dot(t0, halves(cat(n2, n1)))))
    first_n = dot(bottom0, halves(cat(n1, n0) - dot(h0, halves(cat(p1, p0)))))
    p_ref[...] = dot(top1, halves(first_p[:, :B] - dot(t1, halves(first_n[:, :B]))))
    n_ref[...] = dot(bottom1, halves(first_n[:, B:] - dot(h1, halves(first_p[:, B:]))))


VMEM = pl.BlockSpec(memory_space=pltpu.VMEM)
SMEM = pl.BlockSpec(memory_space=pltpu.SMEM)
ANY = pl.BlockSpec(memory_space=pl.ANY)


def resident(*arrays):
    return [pltpu.with_memory_space_constraint(a, pltpu.VMEM) for a in arrays]


def send(array, pairs):
    return lax.ppermute(array, AXIS, pairs)


def steps(positive_row, negative_row):
    me = lax.axis_index(AXIS)
    devices = lax.axis_size(AXIS)
    cores = [[i, i + 1] for i in range(0, devices, 2)]
    onward = [(i, i + 1) for i in range(1, devices - 1)]
    own = pl.pallas_call(
        stack_kernel,
        out_shape=pltpu.VMEM((2 * B, B), jnp.float32),
        in_specs=[ANY] * 2,
        out_specs=VMEM,
        scratch_shapes=[pltpu.SemaphoreType.DMA((2,))],
    )(positive_row, negative_row)
    second = send(own, [(0, 1), (1, 0)])
    back1 = send(own, onward)
    held = pl.pallas_call(
        factor_kernel,
        out_shape=pltpu.VMEM((B, B), jnp.float32),
        in_specs=[SMEM, VMEM, VMEM],
        out_specs=VMEM,
    )(jnp.reshape(me, (1,)).astype(jnp.int32), *resident(own, second))

    back2 = send(jnp.where(me == 0, own, back1), [(0, 2)] + onward[1:])
    back1 = jnp.where(me == 1, second, back1)
    rounds = tree_rounds()
    for permutes in rounds:
        arrived = [send(held, pairs) for pairs in permutes]
        for block in arrived:
            held = held + block

    both = lax.all_gather(held, AXIS, axis=0, axis_index_groups=cores)
    return pl.pallas_call(
        apply_kernel,
        out_shape=[jax.ShapeDtypeStruct((B, B), jnp.float32)] * 2,
        in_specs=[VMEM] * 4,
        out_specs=[VMEM] * 2,
    )(*resident(both, back2, back1, own))


def solution(mesh):
    spec = P(None, AXIS)
    return jax.shard_map(
        steps, mesh=mesh, in_specs=(spec, spec), out_specs=(spec, spec), check_vma=False
    )
```

```python
import jax
import jax.numpy as jnp
from jax import lax
from jax.experimental import pallas as pl
from jax.experimental.pallas import tpu as pltpu
from jax.sharding import PartitionSpec as P


B = 256
AXIS = "blk"

XS, ZS, YS = 4, 8, 8


def position(x, z, y, core):
    return (((x % XS) * ZS + z % ZS) * YS + y % YS) * 2 + core


TREE = (
    (
        ((0, 0, 2), (0, 0, -2), (0, 0, 4)),
        ((1, 0, 0), (2, 0, 0), (-1, 0, 0)),
        ((0, 4, 0), (0, 0, -1), (0, 4, -1)),
        ((0, 1, 0), (0, 2, 0), (0, -1, 0)),
    ),
    (
        ((2, 0, 0), (-1, 0, 0), (1, 0, 0)),
        ((0, 0, 2), (0, 0, -2), (0, 0, 4)),
        ((0, -2, 0), (0, 2, 0), (0, 4, 0)),
        ((0, 0, 1), (0, -1, 0), (0, -1, 1)),
    ),
)


def tree_rounds():
    holders = [[(0, 0, 0)], [(0, 0, 0)]]
    rounds = []
    for r in range(len(TREE[0])):
        permutes = []
        fresh = [[], []]
        for k in range(len(TREE[0][r])):
            pairs = []
            for core in range(2):
                dx, dz, dy = TREE[core][r][k]
                for x, z, y in holders[core]:
                    to = ((x + dx) % XS, (z + dz) % ZS, (y + dy) % YS)
                    fresh[core].append(to)
                    pairs.append((position(x, z, y, core), position(*to, core)))
            permutes.append(pairs)
        for core in range(2):
            holders[core] += fresh[core]
        rounds.append(permutes)
    return rounds


def halves(a):
    high = a.astype(jnp.bfloat16)
    low = (a - high.astype(jnp.float32)).astype(jnp.bfloat16)
    return high, low


def dot(a, b):
    rows = a[0].shape[0]
    both = jnp.dot(jnp.concatenate([a[0], a[1]], axis=0), b[0], preferred_element_type=jnp.float32)
    cross = jnp.dot(a[0], b[1], preferred_element_type=jnp.float32)
    return both[:rows] + (both[rows:] + cross)


def eye():
    rows = lax.broadcasted_iota(jnp.int32, (B, B), 0)
    cols = lax.broadcasted_iota(jnp.int32, (B, B), 1)
    return jnp.where(rows == cols, 1.0, 0.0).astype(jnp.float32)


def coupling_of(lead_p, lead_n, identity):
    diag = jnp.sum(lead_p * identity, axis=1, keepdims=True)
    w1 = identity - lead_p * (1.0 / diag)
    h1 = halves(w1)
    w2 = dot(h1, h1)
    m1 = lead_n + dot(halves(lead_n), h1)
    h2 = halves(w2)
    w4 = dot(h2, h2)
    m2 = m1 + dot(halves(m1), h2)
    h4 = halves(w4)
    w8 = dot(h4, h4)
    m3 = m2 + dot(halves(m2), h4)
    m4 = m3 + dot(halves(m3), halves(w8))
    diag_row = jnp.sum(lead_p * identity, axis=0, keepdims=True)
    return m4 * (1.0 / diag_row)


def root_of(gram, identity):
    e = halves(gram)
    square = dot(e, e)
    inner = 0.375 * identity + 0.3125 * gram + 0.2734375 * square
    return identity + 0.5 * gram + dot(halves(square), halves(inner))


def roots_of(k, kt, identity):
    top = root_of(dot(kt, k), identity)
    bottom = root_of(dot(k, kt), identity)
    return halves(top), halves(bottom)


def stack_kernel(p_ref, n_ref, out_ref, sems):
    copies = [
        pltpu.make_async_copy(p_ref, out_ref.at[:B, :], sems.at[0]),
        pltpu.make_async_copy(n_ref, out_ref.at[B:, :], sems.at[1]),
    ]
    for copy in copies:
        copy.start()
    for copy in copies:
        copy.wait()


def factor_kernel(me_ref, own_ref, other_ref, out_ref):
    me = me_ref[0]

    @pl.when(me >= 2)
    def _():
        out_ref[...] = jnp.zeros_like(out_ref)

    @pl.when(me < 2)
    def _():
        identity = eye()
        mine, other = own_ref[...], other_ref[...]
        first, second = jnp.where(me == 0, mine, other), jnp.where(me == 0, other, mine)
        p0, n0, p1, n1 = first[:B, :], first[B:, :], second[:B, :], second[B:, :]
        k0 = coupling_of(p0, n0, identity)
        k, kt = halves(k0), halves(k0.T)
        top, bottom = roots_of(k, kt, identity)
        lead_p = dot(top, halves(p0 - dot(kt, halves(n0))))
        lead_n = dot(bottom, halves(n1 - dot(k, halves(p1))))
        k1 = coupling_of(lead_p, lead_n, identity)
        out_ref[...] = jnp.where(me == 0, k0, k1)


def apply_kernel(k_ref, back2_ref, back1_ref, own_ref, p_ref, n_ref):
    identity = eye()
    k0, k1 = k_ref[0], k_ref[1]
    h0, t0 = halves(k0), halves(k0.T)
    h1, t1 = halves(k1), halves(k1.T)
    top0, bottom0 = roots_of(h0, t0, identity)
    top1, bottom1 = roots_of(h1, t1, identity)
    p2, n2 = back2_ref[:B, :], back2_ref[B:, :]
    p1, n1 = back1_ref[:B, :], back1_ref[B:, :]
    p0, n0 = own_ref[:B, :], own_ref[B:, :]
    cat = lambda a, b: jnp.concatenate([a, b], axis=1)
    first_p = dot(top0, halves(cat(p2, p1) - dot(t0, halves(cat(n2, n1)))))
    first_n = dot(bottom0, halves(cat(n1, n0) - dot(h0, halves(cat(p1, p0)))))
    p_ref[...] = dot(top1, halves(first_p[:, :B] - dot(t1, halves(first_n[:, :B]))))
    n_ref[...] = dot(bottom1, halves(first_n[:, B:] - dot(h1, halves(first_p[:, B:]))))


VMEM = pl.BlockSpec(memory_space=pltpu.VMEM)
SMEM = pl.BlockSpec(memory_space=pltpu.SMEM)
ANY = pl.BlockSpec(memory_space=pl.ANY)


def resident(*arrays):
    return [pltpu.with_memory_space_constraint(a, pltpu.VMEM) for a in arrays]


def send(array, pairs):
    return lax.ppermute(array, AXIS, pairs)


def steps(positive_row, negative_row):
    me = lax.axis_index(AXIS)
    devices = lax.axis_size(AXIS)
    cores = [[i, i + 1] for i in range(0, devices, 2)]
    onward = [(i, i + 1) for i in range(1, devices - 1)]
    own = pl.pallas_call(
        stack_kernel,
        out_shape=pltpu.VMEM((2 * B, B), jnp.float32),
        in_specs=[ANY] * 2,
        out_specs=VMEM,
        scratch_shapes=[pltpu.SemaphoreType.DMA((2,))],
    )(positive_row, negative_row)
    second = send(own, [(0, 1), (1, 0)])
    back1 = send(own, onward)
    held = pl.pallas_call(
        factor_kernel,
        out_shape=pltpu.VMEM((B, B), jnp.float32),
        in_specs=[SMEM, VMEM, VMEM],
        out_specs=VMEM,
    )(jnp.reshape(me, (1,)).astype(jnp.int32), *resident(own, second))

    back2 = send(jnp.where(me == 0, own, back1), [(0, 2)] + onward[1:])
    back1 = jnp.where(me == 1, second, back1)
    rounds = tree_rounds()
    for permutes in rounds:
        arrived = [send(held, pairs) for pairs in permutes]
        for block in arrived:
            held = held + block

    both = lax.all_gather(held, AXIS, axis=0, axis_index_groups=cores)
    return pl.pallas_call(
        apply_kernel,
        out_shape=[jax.ShapeDtypeStruct((B, B), jnp.float32)] * 2,
        in_specs=[VMEM] * 4,
        out_specs=[VMEM] * 2,
    )(*resident(both, back2, back1, own))


def solution(mesh):
    spec = P(None, AXIS)
    return jax.shard_map(
        steps, mesh=mesh, in_specs=(spec, spec), out_specs=(spec, spec), check_vma=False
    )
```

```python
import jax
import jax.numpy as jnp
from jax import lax
from jax.experimental import pallas as pl
from jax.experimental.pallas import tpu as pltpu
from jax.sharding import PartitionSpec as P


B = 256
AXIS = "blk"

XS, ZS, YS = 4, 8, 8


def position(x, z, y, core):
    return (((x % XS) * ZS + z % ZS) * YS + y % YS) * 2 + core


TREE = (
    (
        ((0, 0, 2), (0, 0, -2), (0, 0, 4)),
        ((0, 0, -1), (0, 2, 0), (0, 2, -1)),
        ((0, 4, 0), (0, 1, 0), (0, -3, 0)),
        ((1, 0, 0), (-1, 0, 0), (2, 0, 0)),
    ),
    (
        ((2, 0, 0), (-1, 0, 0), (1, 0, 0)),
        ((0, 0, 2), (0, 0, -2), (0, 0, 4)),
        ((0, 2, 0), (0, -2, 0), (0, 4, 0)),
        ((0, 0, 1), (0, -1, 0), (0, -1, 1)),
    ),
)


def tree_rounds():
    holders = [[(0, 0, 0)], [(0, 0, 0)]]
    rounds = []
    for r in range(len(TREE[0])):
        permutes = []
        fresh = [[], []]
        for k in range(len(TREE[0][r])):
            pairs = []
            for core in range(2):
                dx, dz, dy = TREE[core][r][k]
                for x, z, y in holders[core]:
                    to = ((x + dx) % XS, (z + dz) % ZS, (y + dy) % YS)
                    fresh[core].append(to)
                    pairs.append((position(x, z, y, core), position(*to, core)))
            permutes.append(pairs)
        for core in range(2):
            holders[core] += fresh[core]
        rounds.append(permutes)
    return rounds


def halves(a):
    high = a.astype(jnp.bfloat16)
    low = (a - high.astype(jnp.float32)).astype(jnp.bfloat16)
    return high, low


def dot(a, b):
    left = jnp.concatenate([a[0], a[0], a[1]], axis=1)
    right = jnp.concatenate([b[0], b[1], b[0]], axis=0)
    return jnp.dot(left, right, preferred_element_type=jnp.float32)


def eye():
    rows = lax.broadcasted_iota(jnp.int32, (B, B), 0)
    cols = lax.broadcasted_iota(jnp.int32, (B, B), 1)
    return jnp.where(rows == cols, 1.0, 0.0).astype(jnp.float32)


def coupling_of(lead_p, lead_n, identity):
    diag = jnp.sum(lead_p * identity, axis=1, keepdims=True)
    w1 = identity - lead_p * (1.0 / diag)
    h1 = halves(w1)
    w2 = dot(h1, h1)
    m1 = lead_n + dot(halves(lead_n), h1)
    h2 = halves(w2)
    w4 = dot(h2, h2)
    m2 = m1 + dot(halves(m1), h2)
    h4 = halves(w4)
    w8 = dot(h4, h4)
    m3 = m2 + dot(halves(m2), h4)
    m4 = m3 + dot(halves(m3), halves(w8))
    diag_row = jnp.sum(lead_p * identity, axis=0, keepdims=True)
    return m4 * (1.0 / diag_row)


def root_of(gram, identity):
    e = halves(gram)
    square = dot(e, e)
    inner = 0.375 * identity + 0.3125 * gram + 0.2734375 * square
    return identity + 0.5 * gram + dot(halves(square), halves(inner))


def roots_of(k, kt, identity):
    top = root_of(dot(kt, k), identity)
    bottom = root_of(dot(k, kt), identity)
    return halves(top), halves(bottom)


def stack_kernel(p_ref, n_ref, out_ref, sems):
    copies = [
        pltpu.make_async_copy(p_ref, out_ref.at[:B, :], sems.at[0]),
        pltpu.make_async_copy(n_ref, out_ref.at[B:, :], sems.at[1]),
    ]
    for copy in copies:
        copy.start()
    for copy in copies:
        copy.wait()


def first_kernel(me_ref, own_ref, out_ref):
    @pl.when(me_ref[0] != 0)
    def _():
        out_ref[...] = jnp.zeros_like(out_ref)

    @pl.when(me_ref[0] == 0)
    def _():
        out_ref[...] = coupling_of(own_ref[:B, :], own_ref[B:, :], eye())


def second_kernel(me_ref, k_ref, own_ref, first_ref, out_ref):
    @pl.when(me_ref[0] != 1)
    def _():
        out_ref[...] = k_ref[...]

    @pl.when(me_ref[0] == 1)
    def _():
        identity = eye()
        p0, n0, p1, n1 = first_ref[:B, :], first_ref[B:, :], own_ref[:B, :], own_ref[B:, :]
        k0 = coupling_of(p0, n0, identity)
        k, kt = halves(k0), halves(k0.T)
        top, bottom = roots_of(k, kt, identity)
        lead_p = dot(top, halves(p0 - dot(kt, halves(n0))))
        lead_n = dot(bottom, halves(n1 - dot(k, halves(p1))))
        out_ref[...] = coupling_of(lead_p, lead_n, identity)


def apply_kernel(k_ref, back2_ref, back1_ref, own_ref, p_ref, n_ref):
    identity = eye()
    k0, k1 = k_ref[0], k_ref[1]
    h0, t0 = halves(k0), halves(k0.T)
    h1, t1 = halves(k1), halves(k1.T)
    top0, bottom0 = roots_of(h0, t0, identity)
    top1, bottom1 = roots_of(h1, t1, identity)
    p2, n2 = back2_ref[:B, :], back2_ref[B:, :]
    p1, n1 = back1_ref[:B, :], back1_ref[B:, :]
    p0, n0 = own_ref[:B, :], own_ref[B:, :]
    cat = lambda a, b: jnp.concatenate([a, b], axis=1)
    first_p = dot(top0, halves(cat(p2, p1) - dot(t0, halves(cat(n2, n1)))))
    first_n = dot(bottom0, halves(cat(n1, n0) - dot(h0, halves(cat(p1, p0)))))
    p_ref[...] = dot(top1, halves(first_p[:, :B] - dot(t1, halves(first_n[:, :B]))))
    n_ref[...] = dot(bottom1, halves(first_n[:, B:] - dot(h1, halves(first_p[:, B:]))))


VMEM = pl.BlockSpec(memory_space=pltpu.VMEM)
SMEM = pl.BlockSpec(memory_space=pltpu.SMEM)
ANY = pl.BlockSpec(memory_space=pl.ANY)


def resident(*arrays):
    return [pltpu.with_memory_space_constraint(a, pltpu.VMEM) for a in arrays]


def send(array, pairs):
    return lax.ppermute(array, AXIS, pairs)


def steps(positive_row, negative_row):
    me = lax.axis_index(AXIS)
    devices = lax.axis_size(AXIS)
    cores = [[i, i + 1] for i in range(0, devices, 2)]
    onward = [(i, i + 1) for i in range(1, devices - 1)]
    own = pl.pallas_call(
        stack_kernel,
        out_shape=pltpu.VMEM((2 * B, B), jnp.float32),
        in_specs=[ANY] * 2,
        out_specs=VMEM,
        scratch_shapes=[pltpu.SemaphoreType.DMA((2,))],
    )(positive_row, negative_row)
    second = send(own, [(0, 1), (1, 0)])
    back1 = send(own, onward)
    place = jnp.reshape(me, (1,)).astype(jnp.int32)
    coupling = pltpu.VMEM((B, B), jnp.float32)
    held = pl.pallas_call(
        first_kernel, out_shape=coupling, in_specs=[SMEM, VMEM], out_specs=VMEM
    )(place, *resident(own))
    held = pl.pallas_call(
        second_kernel, out_shape=coupling, in_specs=[SMEM] + [VMEM] * 3, out_specs=VMEM
    )(place, *resident(held, own, second))

    back2 = send(jnp.where(me == 0, own, back1), [(0, 2)] + onward[1:])
    back1 = jnp.where(me == 1, second, back1)
    rounds = tree_rounds()
    for permutes in rounds:
        arrived = [send(held, pairs) for pairs in permutes]
        for block in arrived:
            held = held + block

    both = lax.all_gather(held, AXIS, axis=0, axis_index_groups=cores)
    return pl.pallas_call(
        apply_kernel,
        out_shape=[jax.ShapeDtypeStruct((B, B), jnp.float32)] * 2,
        in_specs=[VMEM] * 4,
        out_specs=[VMEM] * 2,
    )(*resident(both, back2, back1, own))


def solution(mesh):
    spec = P(None, AXIS)
    return jax.shard_map(
        steps, mesh=mesh, in_specs=(spec, spec), out_specs=(spec, spec), check_vma=False
    )
```

```python
import jax
import jax.numpy as jnp
from jax import lax
from jax.experimental import pallas as pl
from jax.experimental.pallas import tpu as pltpu
from jax.sharding import PartitionSpec as P


B = 256
AXIS = "blk"

XS, ZS, YS = 4, 8, 8


def position(x, z, y, core):
    return (((x % XS) * ZS + z % ZS) * YS + y % YS) * 2 + core


TREE = (
    (
        ((0, 0, 2), (0, 0, -2), (0, 0, 4)),
        ((0, 2, 0), (0, -2, 0), (0, 4, 0)),
        ((1, 0, 0), (-1, 0, 0), (2, 0, 0)),
        ((0, 0, -1), (0, 1, 0), (0, 1, -1)),
    ),
    (
        ((2, 0, 0), (-1, 0, 0), (1, 0, 0)),
        ((0, 0, 2), (0, 0, -2), (0, 0, 4)),
        ((0, 2, 0), (0, -2, 0), (0, 4, 0)),
        ((0, 0, 1), (0, -1, 0), (0, -1, 1)),
    ),
)


def tree_rounds():
    holders = [[(0, 0, 0)], [(0, 0, 0)]]
    rounds = []
    for r in range(len(TREE[0])):
        permutes = []
        fresh = [[], []]
        for k in range(len(TREE[0][r])):
            pairs = []
            for core in range(2):
                dx, dz, dy = TREE[core][r][k]
                for x, z, y in holders[core]:
                    to = ((x + dx) % XS, (z + dz) % ZS, (y + dy) % YS)
                    fresh[core].append(to)
                    pairs.append((position(x, z, y, core), position(*to, core)))
            permutes.append(pairs)
        for core in range(2):
            holders[core] += fresh[core]
        rounds.append(permutes)
    return rounds


def halves(a):
    high = a.astype(jnp.bfloat16)
    low = (a - high.astype(jnp.float32)).astype(jnp.bfloat16)
    return high, low


def dot(a, b):
    left = jnp.concatenate([a[0], a[0], a[1]], axis=1)
    right = jnp.concatenate([b[0], b[1], b[0]], axis=0)
    return jnp.dot(left, right, preferred_element_type=jnp.float32)


def eye():
    rows = lax.broadcasted_iota(jnp.int32, (B, B), 0)
    cols = lax.broadcasted_iota(jnp.int32, (B, B), 1)
    return jnp.where(rows == cols, 1.0, 0.0).astype(jnp.float32)


def coupling_of(lead_p, lead_n, identity):
    diag = jnp.sum(lead_p * identity, axis=1, keepdims=True)
    w1 = identity - lead_p * (1.0 / diag)
    h1 = halves(w1)
    w2 = dot(h1, h1)
    m1 = lead_n + dot(halves(lead_n), h1)
    h2 = halves(w2)
    w4 = dot(h2, h2)
    m2 = m1 + dot(halves(m1), h2)
    h4 = halves(w4)
    w8 = dot(h4, h4)
    m3 = m2 + dot(halves(m2), h4)
    m4 = m3 + dot(halves(m3), halves(w8))
    diag_row = jnp.sum(lead_p * identity, axis=0, keepdims=True)
    return m4 * (1.0 / diag_row)


def root_of(gram, identity):
    e = halves(gram)
    square = dot(e, e)
    inner = 0.375 * identity + 0.3125 * gram + 0.2734375 * square
    return identity + 0.5 * gram + dot(halves(square), halves(inner))


def roots_of(k, kt, identity):
    top = root_of(dot(kt, k), identity)
    bottom = root_of(dot(k, kt), identity)
    return halves(top), halves(bottom)


def stack_kernel(p_ref, n_ref, out_ref, sems):
    copies = [
        pltpu.make_async_copy(p_ref, out_ref.at[:B, :], sems.at[0]),
        pltpu.make_async_copy(n_ref, out_ref.at[B:, :], sems.at[1]),
    ]
    for copy in copies:
        copy.start()
    for copy in copies:
        copy.wait()


def first_kernel(me_ref, own_ref, out_ref):
    @pl.when(me_ref[0] != 0)
    def _():
        out_ref[...] = jnp.zeros_like(out_ref)

    @pl.when(me_ref[0] == 0)
    def _():
        out_ref[...] = coupling_of(own_ref[:B, :], own_ref[B:, :], eye())


def second_kernel(me_ref, k_ref, own_ref, first_ref, out_ref):
    @pl.when(me_ref[0] != 1)
    def _():
        out_ref[...] = k_ref[...]

    @pl.when(me_ref[0] == 1)
    def _():
        identity = eye()
        p0, n0, p1, n1 = first_ref[:B, :], first_ref[B:, :], own_ref[:B, :], own_ref[B:, :]
        k0 = coupling_of(p0, n0, identity)
        k, kt = halves(k0), halves(k0.T)
        top, bottom = roots_of(k, kt, identity)
        lead_p = dot(top, halves(p0 - dot(kt, halves(n0))))
        lead_n = dot(bottom, halves(n1 - dot(k, halves(p1))))
        out_ref[...] = coupling_of(lead_p, lead_n, identity)


def apply_kernel(k_ref, back2_ref, back1_ref, own_ref, p_ref, n_ref):
    identity = eye()
    k0, k1 = k_ref[0], k_ref[1]
    h0, t0 = halves(k0), halves(k0.T)
    h1, t1 = halves(k1), halves(k1.T)
    top0, bottom0 = roots_of(h0, t0, identity)
    top1, bottom1 = roots_of(h1, t1, identity)
    p2, n2 = back2_ref[:B, :], back2_ref[B:, :]
    p1, n1 = back1_ref[:B, :], back1_ref[B:, :]
    p0, n0 = own_ref[:B, :], own_ref[B:, :]
    cat = lambda a, b: jnp.concatenate([a, b], axis=1)
    first_p = dot(top0, halves(cat(p2, p1) - dot(t0, halves(cat(n2, n1)))))
    first_n = dot(bottom0, halves(cat(n1, n0) - dot(h0, halves(cat(p1, p0)))))
    p_ref[...] = dot(top1, halves(first_p[:, :B] - dot(t1, halves(first_n[:, :B]))))
    n_ref[...] = dot(bottom1, halves(first_n[:, B:] - dot(h1, halves(first_p[:, B:]))))


VMEM = pl.BlockSpec(memory_space=pltpu.VMEM)
SMEM = pl.BlockSpec(memory_space=pltpu.SMEM)
ANY = pl.BlockSpec(memory_space=pl.ANY)


def resident(*arrays):
    return [pltpu.with_memory_space_constraint(a, pltpu.VMEM) for a in arrays]


def send(array, pairs):
    return lax.ppermute(array, AXIS, pairs)


def steps(positive_row, negative_row):
    me = lax.axis_index(AXIS)
    devices = lax.axis_size(AXIS)
    cores = [[i, i + 1] for i in range(0, devices, 2)]
    onward = [(i, i + 1) for i in range(1, devices - 1)]
    own = pl.pallas_call(
        stack_kernel,
        out_shape=pltpu.VMEM((2 * B, B), jnp.float32),
        in_specs=[ANY] * 2,
        out_specs=VMEM,
        scratch_shapes=[pltpu.SemaphoreType.DMA((2,))],
    )(positive_row, negative_row)
    second = send(own, [(0, 1), (1, 0)])
    back1 = send(own, onward)
    place = jnp.reshape(me, (1,)).astype(jnp.int32)
    coupling = pltpu.VMEM((B, B), jnp.float32)
    held = pl.pallas_call(
        first_kernel, out_shape=coupling, in_specs=[SMEM, VMEM], out_specs=VMEM
    )(place, *resident(own))
    held = pl.pallas_call(
        second_kernel, out_shape=coupling, in_specs=[SMEM] + [VMEM] * 3, out_specs=VMEM
    )(place, *resident(held, own, second))

    back1 = jnp.where(me == 1, second, back1)
    back2 = send(back1, onward)
    rounds = tree_rounds()
    for permutes in rounds:
        arrived = [send(held, pairs) for pairs in permutes]
        for block in arrived:
            held = held + block

    both = lax.all_gather(held, AXIS, axis=0, axis_index_groups=cores)
    return pl.pallas_call(
        apply_kernel,
        out_shape=[jax.ShapeDtypeStruct((B, B), jnp.float32)] * 2,
        in_specs=[VMEM] * 4,
        out_specs=[VMEM] * 2,
    )(*resident(both, back2, back1, own))


def solution(mesh):
    spec = P(None, AXIS)
    return jax.shard_map(
        steps, mesh=mesh, in_specs=(spec, spec), out_specs=(spec, spec), check_vma=False
    )
```

```python
import jax
import jax.numpy as jnp
from jax import lax
from jax.experimental import pallas as pl
from jax.experimental.pallas import tpu as pltpu
from jax.sharding import PartitionSpec as P


B = 256
AXIS = "blk"

XS, ZS, YS = 4, 8, 8


def position(x, z, y, core):
    return (((x % XS) * ZS + z % ZS) * YS + y % YS) * 2 + core


TREE = (
    (
        ((0, 0, 4), (0, 0, -2), (0, 0, 2)),
        ((0, 2, 0), (0, 4, 0), (0, -2, 0)),
        ((1, 0, 0), (-1, 0, 0), (2, 0, 0)),
        ((0, 0, -1), (0, 1, 0), (0, 1, -1)),
    ),
    (
        ((2, 0, 0), (-1, 0, 0), (1, 0, 0)),
        ((0, 0, 2), (0, 0, -2), (0, 0, 4)),
        ((0, 2, 0), (0, -2, 0), (0, 4, 0)),
        ((0, 0, 1), (0, -1, 0), (0, -1, 1)),
    ),
)


def tree_rounds():
    holders = [[(0, 0, 0)], [(0, 0, 0)]]
    rounds = []
    for r in range(len(TREE[0])):
        permutes = []
        fresh = [[], []]
        for k in range(len(TREE[0][r])):
            pairs = []
            for core in range(2):
                dx, dz, dy = TREE[core][r][k]
                for x, z, y in holders[core]:
                    to = ((x + dx) % XS, (z + dz) % ZS, (y + dy) % YS)
                    fresh[core].append(to)
                    pairs.append((position(x, z, y, core), position(*to, core)))
            permutes.append(pairs)
        for core in range(2):
            holders[core] += fresh[core]
        rounds.append(permutes)
    return rounds


def halves(a):
    high = a.astype(jnp.bfloat16)
    low = (a - high.astype(jnp.float32)).astype(jnp.bfloat16)
    return high, low


def dot(a, b):
    left = jnp.concatenate([a[0], a[0], a[1]], axis=1)
    right = jnp.concatenate([b[0], b[1], b[0]], axis=0)
    return jnp.dot(left, right, preferred_element_type=jnp.float32)


def eye():
    rows = lax.broadcasted_iota(jnp.int32, (B, B), 0)
    cols = lax.broadcasted_iota(jnp.int32, (B, B), 1)
    return jnp.where(rows == cols, 1.0, 0.0).astype(jnp.float32)


def coupling_of(lead_p, lead_n, identity):
    diag = jnp.sum(lead_p * identity, axis=1, keepdims=True)
    w1 = identity - lead_p * (1.0 / diag)
    h1 = halves(w1)
    w2 = dot(h1, h1)
    m1 = lead_n + dot(halves(lead_n), h1)
    h2 = halves(w2)
    w4 = dot(h2, h2)
    m2 = m1 + dot(halves(m1), h2)
    h4 = halves(w4)
    w8 = dot(h4, h4)
    m3 = m2 + dot(halves(m2), h4)
    m4 = m3 + dot(halves(m3), halves(w8))
    diag_row = jnp.sum(lead_p * identity, axis=0, keepdims=True)
    return m4 * (1.0 / diag_row)


def root_of(gram, identity):
    e = halves(gram)
    square = dot(e, e)
    inner = 0.375 * identity + 0.3125 * gram + 0.2734375 * square
    return identity + 0.5 * gram + dot(halves(square), halves(inner))


def roots_of(k, kt, identity):
    top = root_of(dot(kt, k), identity)
    bottom = root_of(dot(k, kt), identity)
    return halves(top), halves(bottom)


def stack_kernel(p_ref, n_ref, out_ref, sems):
    copies = [
        pltpu.make_async_copy(p_ref, out_ref.at[:B, :], sems.at[0]),
        pltpu.make_async_copy(n_ref, out_ref.at[B:, :], sems.at[1]),
    ]
    for copy in copies:
        copy.start()
    for copy in copies:
        copy.wait()


def factor_kernel(me_ref, own_ref, other_ref, out_ref):
    me = me_ref[0]

    @pl.when(me >= 2)
    def _():
        out_ref[...] = jnp.zeros_like(out_ref)

    @pl.when(me < 2)
    def _():
        identity = eye()
        mine, other = own_ref[...], other_ref[...]
        first, second = jnp.where(me == 0, mine, other), jnp.where(me == 0, other, mine)
        p0, n0, p1, n1 = first[:B, :], first[B:, :], second[:B, :], second[B:, :]
        k0 = coupling_of(p0, n0, identity)
        k, kt = halves(k0), halves(k0.T)
        top, bottom = roots_of(k, kt, identity)
        lead_p = dot(top, halves(p0 - dot(kt, halves(n0))))
        lead_n = dot(bottom, halves(n1 - dot(k, halves(p1))))
        k1 = coupling_of(lead_p, lead_n, identity)
        out_ref[...] = jnp.where(me == 0, k0, k1)


def apply_kernel(k_ref, back2_ref, back1_ref, own_ref, p_ref, n_ref):
    identity = eye()
    k0, k1 = k_ref[0], k_ref[1]
    h0, t0 = halves(k0), halves(k0.T)
    h1, t1 = halves(k1), halves(k1.T)
    top0, bottom0 = roots_of(h0, t0, identity)
    top1, bottom1 = roots_of(h1, t1, identity)
    p2, n2 = back2_ref[:B, :], back2_ref[B:, :]
    p1, n1 = back1_ref[:B, :], back1_ref[B:, :]
    p0, n0 = own_ref[:B, :], own_ref[B:, :]
    cat = lambda a, b: jnp.concatenate([a, b], axis=1)
    first_p = dot(top0, halves(cat(p2, p1) - dot(t0, halves(cat(n2, n1)))))
    first_n = dot(bottom0, halves(cat(n1, n0) - dot(h0, halves(cat(p1, p0)))))
    p_ref[...] = dot(top1, halves(first_p[:, :B] - dot(t1, halves(first_n[:, :B]))))
    n_ref[...] = dot(bottom1, halves(first_n[:, B:] - dot(h1, halves(first_p[:, B:]))))


VMEM = pl.BlockSpec(memory_space=pltpu.VMEM)
SMEM = pl.BlockSpec(memory_space=pltpu.SMEM)
ANY = pl.BlockSpec(memory_space=pl.ANY)


def resident(*arrays):
    return [pltpu.with_memory_space_constraint(a, pltpu.VMEM) for a in arrays]


def send(array, pairs):
    return lax.ppermute(array, AXIS, pairs)


def steps(positive_row, negative_row):
    me = lax.axis_index(AXIS)
    devices = lax.axis_size(AXIS)
    cores = [[i, i + 1] for i in range(0, devices, 2)]
    onward = [(i, i + 1) for i in range(1, devices - 1)]
    own = pl.pallas_call(
        stack_kernel,
        out_shape=pltpu.VMEM((2 * B, B), jnp.float32),
        in_specs=[ANY] * 2,
        out_specs=VMEM,
        scratch_shapes=[pltpu.SemaphoreType.DMA((2,))],
    )(positive_row, negative_row)
    second = send(own, [(0, 1), (1, 0)])
    back1 = send(own, onward)
    held = pl.pallas_call(
        factor_kernel,
        out_shape=pltpu.VMEM((B, B), jnp.float32),
        in_specs=[SMEM, VMEM, VMEM],
        out_specs=VMEM,
    )(jnp.reshape(me, (1,)).astype(jnp.int32), *resident(own, second))

    back2 = send(jnp.where(me == 0, own, back1), [(0, 2)] + onward[1:])
    back1 = jnp.where(me == 1, second, back1)
    rounds = tree_rounds()
    for permutes in rounds:
        arrived = [send(held, pairs) for pairs in permutes]
        for block in arrived:
            held = held + block

    both = lax.all_gather(held, AXIS, axis=0, axis_index_groups=cores)
    return pl.pallas_call(
        apply_kernel,
        out_shape=[jax.ShapeDtypeStruct((B, B), jnp.float32)] * 2,
        in_specs=[VMEM] * 4,
        out_specs=[VMEM] * 2,
    )(*resident(both, back2, back1, own))


def solution(mesh):
    spec = P(None, AXIS)
    return jax.shard_map(
        steps, mesh=mesh, in_specs=(spec, spec), out_specs=(spec, spec), check_vma=False
    )
```

```python
import jax
import jax.numpy as jnp
from jax import lax
from jax.experimental import pallas as pl
from jax.experimental.pallas import tpu as pltpu
from jax.sharding import PartitionSpec as P


B = 256
AXIS = "blk"

XS, ZS, YS = 4, 8, 8


def position(x, z, y, core):
    return (((x % XS) * ZS + z % ZS) * YS + y % YS) * 2 + core


TREE = (
    (
        ((0, 0, 4), (0, 0, -2), (0, 0, 2)),
        ((0, 2, 0), (0, 4, 0), (0, -2, 0)),
        ((1, 0, 0), (-1, 0, 0), (2, 0, 0)),
        ((0, 0, -1), (0, 1, 0), (0, 1, -1)),
    ),
    (
        ((2, 0, 0), (-1, 0, 0), (1, 0, 0)),
        ((0, 0, 2), (0, 0, -2), (0, 0, 4)),
        ((0, 2, 0), (0, -2, 0), (0, 4, 0)),
        ((0, 0, 1), (0, -1, 0), (0, -1, 1)),
    ),
)


def tree_rounds():
    holders = [[(0, 0, 0)], [(0, 0, 0)]]
    rounds = []
    for r in range(len(TREE[0])):
        permutes = []
        fresh = [[], []]
        for k in range(len(TREE[0][r])):
            pairs = []
            for core in range(2):
                dx, dz, dy = TREE[core][r][k]
                for x, z, y in holders[core]:
                    to = ((x + dx) % XS, (z + dz) % ZS, (y + dy) % YS)
                    fresh[core].append(to)
                    pairs.append((position(x, z, y, core), position(*to, core)))
            permutes.append(pairs)
        for core in range(2):
            holders[core] += fresh[core]
        rounds.append(permutes)
    return rounds


def halves(a):
    high = a.astype(jnp.bfloat16)
    low = (a - high.astype(jnp.float32)).astype(jnp.bfloat16)
    return high, low


def dot(a, b):
    rows = a[0].shape[0]
    both = jnp.dot(jnp.concatenate([a[0], a[1]], axis=0), b[0], preferred_element_type=jnp.float32)
    cross = jnp.dot(a[0], b[1], preferred_element_type=jnp.float32)
    return both[:rows] + (both[rows:] + cross)


def eye():
    rows = lax.broadcasted_iota(jnp.int32, (B, B), 0)
    cols = lax.broadcasted_iota(jnp.int32, (B, B), 1)
    return jnp.where(rows == cols, 1.0, 0.0).astype(jnp.float32)


def coupling_of(lead_p, lead_n, identity):
    diag = jnp.sum(lead_p * identity, axis=1, keepdims=True)
    w1 = identity - lead_p * (1.0 / diag)
    h1 = halves(w1)
    w2 = dot(h1, h1)
    m1 = lead_n + dot(halves(lead_n), h1)
    h2 = halves(w2)
    w4 = dot(h2, h2)
    m2 = m1 + dot(halves(m1), h2)
    h4 = halves(w4)
    w8 = dot(h4, h4)
    m3 = m2 + dot(halves(m2), h4)
    m4 = m3 + dot(halves(m3), halves(w8))
    diag_row = jnp.sum(lead_p * identity, axis=0, keepdims=True)
    return m4 * (1.0 / diag_row)


def root_of(gram, identity):
    e = halves(gram)
    square = dot(e, e)
    inner = 0.375 * identity + 0.3125 * gram + 0.2734375 * square
    return identity + 0.5 * gram + dot(halves(square), halves(inner))


def roots_of(k, kt, identity):
    top = root_of(dot(kt, k), identity)
    bottom = root_of(dot(k, kt), identity)
    return halves(top), halves(bottom)


def stack_kernel(p_ref, n_ref, out_ref, sems):
    copies = [
        pltpu.make_async_copy(p_ref, out_ref.at[:B, :], sems.at[0]),
        pltpu.make_async_copy(n_ref, out_ref.at[B:, :], sems.at[1]),
    ]
    for copy in copies:
        copy.start()
    for copy in copies:
        copy.wait()


def factor_kernel(me_ref, own_ref, other_ref, out_ref):
    me = me_ref[0]

    @pl.when(me >= 2)
    def _():
        out_ref[...] = jnp.zeros_like(out_ref)

    @pl.when(me < 2)
    def _():
        identity = eye()
        mine, other = own_ref[...], other_ref[...]
        first, second = jnp.where(me == 0, mine, other), jnp.where(me == 0, other, mine)
        p0, n0, p1, n1 = first[:B, :], first[B:, :], second[:B, :], second[B:, :]
        k0 = coupling_of(p0, n0, identity)
        k, kt = halves(k0), halves(k0.T)
        top, bottom = roots_of(k, kt, identity)
        lead_p = dot(top, halves(p0 - dot(kt, halves(n0))))
        lead_n = dot(bottom, halves(n1 - dot(k, halves(p1))))
        k1 = coupling_of(lead_p, lead_n, identity)
        out_ref[...] = jnp.where(me == 0, k0, k1)


def apply_kernel(k_ref, back2_ref, back1_ref, own_ref, p_ref, n_ref, p_buf, n_buf, sems):
    identity = eye()
    k0, k1 = k_ref[0], k_ref[1]
    h0, t0 = halves(k0), halves(k0.T)
    h1, t1 = halves(k1), halves(k1.T)
    top0, bottom0 = roots_of(h0, t0, identity)
    top1, bottom1 = roots_of(h1, t1, identity)
    p2, n2 = back2_ref[:B, :], back2_ref[B:, :]
    p1, n1 = back1_ref[:B, :], back1_ref[B:, :]
    p0, n0 = own_ref[:B, :], own_ref[B:, :]
    cat = lambda a, b: jnp.concatenate([a, b], axis=1)
    first_p = dot(top0, halves(cat(p2, p1) - dot(t0, halves(cat(n2, n1)))))
    first_n = dot(bottom0, halves(cat(n1, n0) - dot(h0, halves(cat(p1, p0)))))
    n_buf[...] = dot(bottom1, halves(first_n[:, B:] - dot(h1, halves(first_p[:, B:]))))
    n_copy = pltpu.make_async_copy(n_buf, n_ref, sems.at[0])
    n_copy.start()
    p_buf[...] = dot(top1, halves(first_p[:, :B] - dot(t1, halves(first_n[:, :B]))))
    p_copy = pltpu.make_async_copy(p_buf, p_ref, sems.at[1])
    p_copy.start()
    n_copy.wait()
    p_copy.wait()


VMEM = pl.BlockSpec(memory_space=pltpu.VMEM)
SMEM = pl.BlockSpec(memory_space=pltpu.SMEM)
ANY = pl.BlockSpec(memory_space=pl.ANY)


def resident(*arrays):
    return [pltpu.with_memory_space_constraint(a, pltpu.VMEM) for a in arrays]


def send(array, pairs):
    return lax.ppermute(array, AXIS, pairs)


def steps(positive_row, negative_row):
    me = lax.axis_index(AXIS)
    devices = lax.axis_size(AXIS)
    cores = [[i, i + 1] for i in range(0, devices, 2)]
    onward = [(i, i + 1) for i in range(1, devices - 1)]
    own = pl.pallas_call(
        stack_kernel,
        out_shape=pltpu.VMEM((2 * B, B), jnp.float32),
        in_specs=[ANY] * 2,
        out_specs=VMEM,
        scratch_shapes=[pltpu.SemaphoreType.DMA((2,))],
    )(positive_row, negative_row)
    second = send(own, [(0, 1), (1, 0)])
    back1 = send(own, onward)
    held = pl.pallas_call(
        factor_kernel,
        out_shape=pltpu.VMEM((B, B), jnp.float32),
        in_specs=[SMEM, VMEM, VMEM],
        out_specs=VMEM,
    )(jnp.reshape(me, (1,)).astype(jnp.int32), *resident(own, second))

    back2 = send(jnp.where(me == 0, own, back1), [(0, 2)] + onward[1:])
    back1 = jnp.where(me == 1, second, back1)
    rounds = tree_rounds()
    for permutes in rounds:
        arrived = [send(held, pairs) for pairs in permutes]
        for block in arrived:
            held = held + block

    both = lax.all_gather(held, AXIS, axis=0, axis_index_groups=cores)
    return pl.pallas_call(
        apply_kernel,
        out_shape=[jax.ShapeDtypeStruct((B, B), jnp.float32)] * 2,
        in_specs=[VMEM] * 4,
        out_specs=[ANY] * 2,
        scratch_shapes=[pltpu.VMEM((B, B), jnp.float32)] * 2 + [pltpu.SemaphoreType.DMA((2,))],
    )(*resident(both, back2, back1, own))


def solution(mesh):
    spec = P(None, AXIS)
    return jax.shard_map(
        steps, mesh=mesh, in_specs=(spec, spec), out_specs=(spec, spec), check_vma=False
    )
```
